32 devices in a mesh: gx: 8 (over y, x, core), gy: 4 (over z).
Axes of the slice: x: 2, y: 2, z: 4, core: 2. Of those that a mesh axis runs over, the one named last changes fastest.
Arguments:
- west_in: float32 [2, 32, 256, 128], P(None, 'gx', 'gy'), may hold values from -6 to 6
- south_in: float32 [2, 256, 16, 128], P(None, 'gx', 'gy'), may hold values from -6 to 6
- region: int32 [256, 256], P('gx', 'gy'), may hold values from 0 to 7
- pml_layers: int32 [4, 8, 4], P(None, 'gx', 'gy'), may hold values from 0 to 8
- vel_table: float32 [8, 128], replicated, may hold values from 0.3 to 3
- src_slot: int32 [8, 4], P('gx', 'gy'), may hold values from 0 to 12
- src_cell: int32 [8, 4], P('gx', 'gy'), may hold values from 0 to 262143
- src_amp: float32 [2, 13], replicated, may hold values from -16 to 16
- wave_sq: float32 [], replicated, may hold values from 0.5 to 2
Outputs:
- fields: bfloat16 [3, 2, 256, 256, 128], P(None, None, 'gx', 'gy')
The draws below stay inside these ranges and needn't reach their ends.
All inputs are finite; a program needn't handle non-finite values.
Results may differ from the reference program's by a relative error of at most 0.001.
Values sent between devices are 32-bit elements; how exact they have to be, the bound alone decides.
A program may use at most 64 MiB of HBM per device.

```python
import math
import jax
import jax.numpy as jnp
from jax import lax

SX = 32
SY = 64
Z = 128
DEPTH = 4
TICKS = 3
REGIONS = 8
NX = 256
NY = 256
NSRC = 13
N_GX = 8
N_GY = 4


def draw_west_in(key, part):
    key_rough = jax.random.fold_in(jax.random.fold_in(key, 11), 0)
    blocks_x = NX // SX
    shape_all = (2, DEPTH * blocks_x, NY, Z)
    values = jax.random.normal(key_rough, shape_all, jnp.float32)
    return jnp.clip(values, -6.0, 6.0)


def draw_south_in(key, part):
    key_rough = jax.random.fold_in(jax.random.fold_in(key, 23), 0)
    blocks_y = NY // SY
    shape_all = (2, NX, DEPTH * blocks_y, Z)
    values = jax.random.normal(key_rough, shape_all, jnp.float32)
    return jnp.clip(values, -6.0, 6.0)


def draw_wave_sq(key, part):
    inner = jax.random.fold_in(key, 37)
    value = jax.random.uniform(inner, (), jnp.float32, 0.5, 2.0)
    return value


def place_ends(drawn, key, low, top_value):
    dims = drawn.shape
    index_at = [jax.random.randint(jax.random.fold_in(key, axis), (), 0, dims[axis]) for axis in range(len(dims))]
    drawn = drawn.at[tuple(index_at)].set(low)
    longest = dims.index(max(dims))
    index_at[longest] = (index_at[longest] + 1) % dims[longest]
    return drawn.at[tuple(index_at)].set(top_value)


def centred(own_key, dims, scale, bound, held_as=jnp.bfloat16):
    values = jax.random.normal(own_key, dims, jnp.float32) * scale
    return jnp.minimum(jnp.maximum(values, -bound), bound).astype(held_as)


def setup_inputs(seed: int = 0) -> dict:
    keys = jax.random.split(jax.random.key(seed), 10)
    west_in = draw_west_in(jax.random.fold_in(keys[9], 71), 0)
    south_in = draw_south_in(jax.random.fold_in(keys[9], 71), 0)
    region = place_ends(jax.random.randint(keys[2], (NX, NY), 0, REGIONS), jax.random.fold_in(keys[2], 1), 0, REGIONS - 1).astype(jnp.int32)
    pml_layers = place_ends(jax.random.randint(keys[3], (4, N_GX, N_GY), 0, 9), jax.random.fold_in(keys[3], 1), 0, 8).astype(jnp.int32)
    vel_table = jnp.clip(jnp.exp(jax.random.uniform(keys[4], (REGIONS, Z), jnp.float32, math.log(0.3), math.log(3.0))), 0.3, 3.0)
    src_slot = place_ends(jax.random.randint(keys[5], (N_GX, N_GY), 0, NSRC), jax.random.fold_in(keys[5], 1), 0, NSRC - 1).astype(jnp.int32)
    src_cell = place_ends(jax.random.randint(keys[6], (N_GX, N_GY), 0, SX * SY * Z), jax.random.fold_in(keys[6], 1), 0, (SX * SY * Z) - 1).astype(jnp.int32)
    src_amp = centred(keys[7], (2, NSRC), 4.0, 16.0, jnp.float32)
    wave_sq = draw_wave_sq(jax.random.fold_in(keys[9], 71), 0)
    return {"west_in": west_in, "south_in": south_in, "region": region, "pml_layers": pml_layers, "vel_table": vel_table, "src_slot": src_slot, "src_cell": src_cell, "src_amp": src_amp, "wave_sq": wave_sq}


precise_mode = lax.Precision.HIGHEST
damping_ratio = 0.25
absorb_peak = 4.0
diagonal_base = 6.0

def tables(count):
    index_vals = jnp.arange(count, dtype=jnp.float32)
    angle_grid = jnp.pi * (index_vals[:, None] + 1.0) * (index_vals[None, :] + 1.0) / (count + 1.0)
    basis_table = jnp.sqrt(2.0 / (count + 1.0)) * jnp.sin(angle_grid)
    eigen_vals = 2.0 - 2.0 * jnp.cos(jnp.pi * (index_vals + 1.0) / (count + 1.0))
    return (basis_table, eigen_vals)

def along_first(field, basis_table):
    return jnp.einsum('kx,cxyz->ckyz', basis_table, field, precision=precise_mode)

def along_second(field, basis_table):
    return jnp.einsum('ky,cxyz->cxkz', basis_table, field, precision=precise_mode)

def along_third(field, basis_table):
    return jnp.einsum('kz,cxyz->cxyk', basis_table, field, precision=precise_mode)

def spectral(forcing, wave_sq, bases):
    basis_x, eigen_x, basis_y, eigen_y, basis_z, eigen_z = bases
    coeffs = along_third(along_second(along_first(forcing, basis_x), basis_y), basis_z)
    shifted = eigen_x[:, None, None] + eigen_y[None, :, None] + eigen_z[None, None, :] - wave_sq
    damping = -damping_ratio * wave_sq
    denominator = shifted * shifted + damping * damping
    real_part = (coeffs[0] * shifted + coeffs[1] * damping) / denominator
    imag_part = (coeffs[1] * shifted - coeffs[0] * damping) / denominator
    return along_third(jnp.stack([real_part, imag_part]), basis_z)

def absorption(layers, size_x, size_y):
    first_pos = jnp.arange(size_x, dtype=jnp.float32)
    second_pos = jnp.arange(size_y, dtype=jnp.float32)

    def ramp(thick, distance):
        portion = jnp.maximum(thick - distance, 0.0) / jnp.maximum(thick, 1.0)
        return portion * portion
    sigma = ramp(layers[0], first_pos)[:, None] + ramp(layers[1], size_x - 1.0 - first_pos)[:, None]
    sigma = sigma + ramp(layers[2], second_pos)[None, :] + ramp(layers[3], size_y - 1.0 - second_pos)[None, :]
    return absorb_peak * sigma

def multipliers(speed_sq, sigma, wave_sq):
    contrast = speed_sq - wave_sq
    denominator = (diagonal_base * diagonal_base + sigma * sigma)[:, :, None]
    mult_real = contrast * diagonal_base / denominator
    mult_imag = -contrast * sigma[:, :, None] / denominator
    return (mult_real, mult_imag)

def correct(field, mult_real, mult_imag):
    real_part = field[0] + mult_real * field[0] - mult_imag * field[1]
    imag_part = field[1] + mult_real * field[1] + mult_imag * field[0]
    return jnp.stack([real_part, imag_part])

def cell_numbers(size_x, size_y, size_z):
    shape_all = (size_x, size_y, size_z)
    first_axis = lax.broadcasted_iota(jnp.int32, shape_all, 0)
    second_axis = lax.broadcasted_iota(jnp.int32, shape_all, 1)
    third_axis = lax.broadcasted_iota(jnp.int32, shape_all, 2)
    return (first_axis * size_y + second_axis) * size_z + third_axis

def build_forcing(west_trace, south_trace, amplitude, live, point_mask, size_x, size_y):
    west_pad = jnp.pad(west_trace, ((0, 0), (0, size_x - DEPTH), (0, 0), (0, 0)))
    south_pad = jnp.pad(south_trace, ((0, 0), (0, 0), (0, size_y - DEPTH), (0, 0)))
    return west_pad + south_pad + amplitude[:, :, None, None] * (live * point_mask)[None]

def block_tick(west_trace, south_trace, labels, layers, slot_value, cell_value, row_index, col_index, tick_index, vel_table, src_amp, wave_sq):
    bases = tables(SX) + tables(SY) + tables(Z)
    speed_sq = jnp.take(vel_table, labels, axis=0)
    sigma = absorption(layers.astype(jnp.float32), SX, SY)
    mult_real, mult_imag = multipliers(speed_sq, sigma, wave_sq)
    source_index = (tick_index - row_index - col_index + N_GX + N_GY - 2).astype(jnp.int32)
    live = (slot_value == source_index).astype(jnp.float32)
    point_mask = (cell_numbers(SX, SY, Z) == cell_value).astype(jnp.float32)
    amplitude = lax.dynamic_slice_in_dim(src_amp, source_index, 1, 1)
    forcing = build_forcing(west_trace, south_trace, amplitude, live, point_mask, SX, SY)
    partial_field = spectral(forcing, wave_sq, bases)
    raw_field = along_first(along_second(partial_field, bases[2]), bases[0])
    return correct(raw_field, mult_real, mult_imag)

def reference(west_in, south_in, region, pml_layers, vel_table, src_slot, src_cell, src_amp, wave_sq):
    west_traces = west_in.reshape(2, N_GX, DEPTH, N_GY, SY, Z).transpose(1, 3, 0, 2, 4, 5)
    south_traces = south_in.reshape(2, N_GX, SX, N_GY, DEPTH, Z).transpose(1, 3, 0, 2, 4, 5)
    label_blocks = region.reshape(N_GX, SX, N_GY, SY).transpose(0, 2, 1, 3)
    layer_blocks = pml_layers.transpose(1, 2, 0)
    row_ids = jnp.arange(N_GX, dtype=jnp.int32)
    col_ids = jnp.arange(N_GY, dtype=jnp.int32)
    results = []
    for tick_index in range(TICKS):

        def one_row(row_items):
            row_index, west_row, south_row, label_row, layer_row, slot_row, cell_row = row_items

            def one_block(col_index, west_block, south_block, label_block, layer_block, slot_value, cell_value):
                field = block_tick(west_block, south_block, label_block, layer_block, slot_value, cell_value, row_index, col_index, tick_index, vel_table, src_amp, wave_sq)
                return (field.astype(jnp.bfloat16), field[:, SX - DEPTH:], field[:, :, SY - DEPTH:])
            return jax.vmap(one_block)(col_ids, west_row, south_row, label_row, layer_row, slot_row, cell_row)
        blocks, east_part, north_part = lax.map(one_row, (row_ids, west_traces, south_traces, label_blocks, layer_blocks, src_slot, src_cell))
        results.append(blocks)
        west_traces = jnp.concatenate([jnp.zeros_like(east_part[:1]), east_part[:-1]], axis=0)
        south_traces = jnp.concatenate([jnp.zeros_like(north_part[:, :1]), north_part[:, :-1]], axis=1)
    stacked = jnp.stack(results)
    return stacked.transpose(0, 3, 1, 4, 2, 5, 6).reshape(TICKS, 2, N_GX * SX, N_GY * SY, Z)
```

```python
import functools

import jax
import jax.numpy as jnp
import numpy as np
from jax import lax
from jax.experimental import pallas as pl
from jax.experimental.pallas import tpu as pltpu
from jax.sharding import PartitionSpec as P

DEPTH = 4
TICKS = 3
PIECES = 4
INNER_PIECES = 3
SUB = 8
damping_ratio = 0.25
absorb_peak = 4.0
diagonal_base = 6.0
F32 = jnp.float32
BF16 = jnp.bfloat16
MESH = pl.DeviceIdType.MESH


def basis(count):
    k = np.arange(count, dtype=np.float64) + 1.0
    table = np.sqrt(2.0 / (count + 1.0)) * np.sin(np.pi * k[:, None] * k[None, :] / (count + 1.0))
    eigen = 2.0 - 2.0 * np.cos(np.pi * k / (count + 1.0))
    return table, eigen


def np_split(table):
    full = np.asarray(table, np.float32)
    high = full.astype(BF16)
    low = (full - high.astype(np.float32)).astype(BF16)
    return high, low


def left3(table):
    high, low = np_split(table)
    return np.concatenate([high, high, low], axis=1)


def fold(table):
    high, low = np_split(table)
    return np.concatenate([np.concatenate([high, high], 1), np.concatenate([low, np.zeros_like(low)], 1)], 0)


def edges_first(table, depth):
    rows = table.shape[0] // 2
    cut = depth * SUB
    return np.concatenate([table[:cut], table[rows:rows + cut], table[cut:rows], table[rows + cut:]], axis=0)


def segments(sx):
    inner = (sx - 2 * DEPTH) // INNER_PIECES
    bounds = [(0, DEPTH), (sx - DEPTH, sx)]
    return bounds + [(DEPTH + k * inner, DEPTH + (k + 1) * inner) for k in range(INNER_PIECES)]


def split(values):
    high = values.astype(BF16).astype(F32)
    return high, values - high


def right3(values):
    high, low = split(values)
    high = high.astype(BF16)
    return jnp.concatenate([high, low.astype(BF16), high], axis=0)


def right2(values):
    high, low = split(values)
    return jnp.concatenate([high.astype(BF16), low.astype(BF16)], axis=0)


def mm(a, b):
    return jnp.dot(a, b, preferred_element_type=F32)


def halves(both):
    size = both.shape[0] // 2
    return both[:size] + both[size:]


def along_z(values, zz):
    high, low = split(values)
    both = jnp.concatenate([high.astype(BF16), low.astype(BF16)], axis=1)
    out = mm(both, zz)
    half = out.shape[1] // 2
    return out[:, :half] + out[:, half:]


def make_tables(sx, sy, sz):
    bx, ex = basis(sx)
    by, ey = basis(sy)
    bz, ez = basis(sz)
    eye = np.eye(SUB)
    groups = sy // SUB
    ls = [np_split(np.kron(np.eye(sx), by[g * SUB:(g + 1) * SUB, :DEPTH])) for g in range(groups)]
    lsh = np.stack([np.concatenate([h, h], axis=1) for h, _ in ls])
    lsl = np.stack([low for _, low in ls])
    half = sx // 2
    order = np.concatenate([np.arange(0, sx, 2), np.arange(1, sx, 2)])
    bxo, exo = bx[order], ex[order]
    lw = left3(np.kron(bxo[:, :DEPTH], eye))
    lw = np.concatenate([lw, np.zeros((lw.shape[0], 4 * SUB), lw.dtype)], axis=1)
    zh, zl = np_split(bz)
    zz = np.concatenate([np.concatenate([zh, zl], 1)] * 2, 0)
    return dict(
        lsh=lsh.reshape(groups // 2, -1, lsh.shape[2]),
        lsl=lsl,
        lw=lw,
        te=edges_first(fold(np.kron(bx[:half, order[:half]], eye)), DEPTH),
        to=edges_first(fold(np.kron(bx[:half, order[half:]], eye)), DEPTH),
        ts=left3(np.kron(bxo, np.eye(DEPTH))),
        ty=fold(by),
        zz=zz,
        bxr=np.repeat(bxo, SUB, axis=0).astype(np.float32),
        byf=by.astype(np.float32),
        bzf=bz.astype(np.float32),
        exr=np.repeat(exo, SUB)[:, None].astype(np.float32) * np.ones((1, sz), np.float32),
        eyr=ey[:, None].astype(np.float32) * np.ones((1, sz), np.float32),
        ezr=ez[None, :].astype(np.float32),
    )


SCALARS = ("pml", "amp", "wave")
INVERSE_UNROLL = 2
NAMES = ("lsh", "lsl", "lw", "te", "to", "ts", "ty", "zz", "bxr", "byf", "bzf", "exr", "eyr", "ezr")


INPUTS = SCALARS + ("west_in", "south_in", "region", "vel") + NAMES
FIRST = ("wave", "ezr", "eyr", "exr", "bxr", "byf", "bzf", "lw", "pml", "region", "vel")
ORDER = FIRST + tuple(name for name in INPUTS if name not in FIRST)


def finish_plane(x, mid, mult, ty):
    sz = mid.shape[3]
    plane = jnp.concatenate([mid[0, x], mid[1, x]], axis=1)
    raw = halves(mm(ty[...], right2(plane)))
    re, im = raw[:, :sz], raw[:, sz:]
    mr, mi = mult[0, x], mult[1, x]
    fr = re + mr * re - mi * im
    fi = im + mr * im + mi * re
    return fr, fi


def finish(early, mid, mult, ty, out, last, sems):
    sx = mid.shape[1]
    count = early.shape[0]
    copies = [pltpu.make_async_copy(early.at[t], out.at[t], sems.at[t]) for t in range(count)]
    for copy in copies:
        copy.start()
    size = sx // PIECES
    for k in range(PIECES):
        for x in range(k * size, (k + 1) * size):
            fr, fi = finish_plane(x, mid, mult, ty)
            last[0, x] = fr.astype(BF16)
            last[1, x] = fi.astype(BF16)
        part = pl.ds(k * size, size)
        copy = pltpu.make_async_copy(last.at[:, part], out.at[count, :, part], sems.at[count + k])
        copy.start()
        copies.append(copy)
    for copy in copies:
        copy.wait()


def kernel(n_gx, n_gy, *refs):
    slot, cell = refs[:2]
    outside, (obuf, mid, mult), refs = refs[2:23], refs[23:26], refs[26:]
    inside, refs = refs[:21], refs[21:]
    pml, amp, wave = inside[:3]
    (west_in, south_in, region, vel,
     lsh, lsl, lw0, te, to, ts, ty, zz, bxr, byf, bzf, exr, eyr, ezr) = inside[3:]
    (
     west_buf, south_buf, east_buf, north_buf,
     lw, point, pq, reg2, ab, rs, wf, sp,
     send_e, recv_w, send_n, recv_s, load_sem) = refs
    sx, sy = region.shape
    sz = vel.shape[1]
    labels = vel.shape[0]
    groups = sy // SUB
    span = sx * SUB
    a = lax.axis_index("gx")
    b = lax.axis_index("gy")
    has_w, has_e = a > 0, a + 1 < n_gx
    has_s, has_n = b > 0, b + 1 < n_gy

    loads = {name: pltpu.make_async_copy(src, dst, load_sem.at[i])
             for i, (name, (src, dst)) in enumerate(zip(INPUTS, zip(outside, inside)))}
    for name in ORDER:
        loads[name].start()

    def need(*names):
        for name in names:
            loads[name].wait()

    barrier = pltpu.get_barrier_semaphore()

    @pl.when(has_w)
    def _():
        pl.semaphore_signal(barrier, inc=1, device_id=(a - 1, b), device_id_type=MESH)

    @pl.when(has_s)
    def _():
        pl.semaphore_signal(barrier, inc=1, device_id=(a, b - 1), device_id_type=MESH)


    @pl.when(jnp.logical_not(has_w))
    def _():
        west_buf[...] = jnp.zeros_like(west_buf)

    @pl.when(jnp.logical_not(has_s))
    def _():
        south_buf[...] = jnp.zeros_like(south_buf)

    need("wave", "exr", "eyr", "ezr")
    w = wave[0, 0]
    damp = -damping_ratio * w

    def inverse_group(g, carry):
        y_part = eyr[pl.ds(pl.multiple_of(g * SUB, SUB), SUB), :]
        lam = exr[...].reshape(sx, SUB, sz) + y_part[None] + ezr[...][None] - w
        lam = lam.reshape(sx * SUB, sz)
        inv = 1.0 / (lam * lam + damp * damp)
        pq[0, g] = lam * inv
        pq[1, g] = damp * inv
        return carry

    lax.fori_loop(0, groups, inverse_group, 0, unroll=INVERSE_UNROLL)
    need("bxr", "byf", "bzf", "lw")

    position = cell[0, 0]
    px = position // (sy * sz)
    py = (position // sz) % sy
    pz = position % sz
    x_lane = lax.broadcasted_iota(jnp.int32, (sx * SUB, sx), 1)
    bxp = jnp.sum(jnp.where(x_lane == px, bxr[...], 0.0), axis=1, keepdims=True)
    y_lane = lax.broadcasted_iota(jnp.int32, (sy, sy), 1)
    byp = jnp.sum(jnp.where(y_lane == py, byf[...], 0.0), axis=1, keepdims=True)
    z_row = lax.broadcasted_iota(jnp.int32, (sz, sz), 0)
    bzp = jnp.sum(jnp.where(z_row == pz, bzf[...], 0.0), axis=0, keepdims=True)
    point[...] = byp * bzp
    width = lw0.shape[1]
    first = 3 * DEPTH * SUB
    lane = lax.broadcasted_iota(jnp.int32, (sx * SUB, width), 1)
    row = lax.broadcasted_iota(jnp.int32, (sx * SUB, width), 0)
    xh, xl = split(bxp)
    dyn = jnp.where(lane < first + 2 * SUB, xh, xl)
    dyn = jnp.where((lane % SUB) == (row % SUB), dyn, 0.0)
    lw[...] = jnp.where(lane < first, lw0[...].astype(F32), dyn).astype(BF16)

    xi = lax.broadcasted_iota(jnp.int32, (sx, 2 * sy), 0).astype(F32)
    lane2 = lax.broadcasted_iota(jnp.int32, (sx, 2 * sy), 1)
    yi = (lane2 % sy).astype(F32)

    need("pml", "region", "vel")

    def ramp(i, distance):
        thick = pml[0, i].astype(F32)
        portion = jnp.maximum(thick - distance, 0.0) / jnp.maximum(jnp.full_like(distance, thick), 1.0)
        return portion * portion

    sigma = ramp(0, xi) + ramp(1, sx - 1.0 - xi) + ramp(2, yi) + ramp(3, sy - 1.0 - yi)
    sigma = absorb_peak * sigma
    den = diagonal_base * diagonal_base + sigma * sigma
    ab[...] = jnp.where(lane2 < sy, diagonal_base, -sigma) / den
    reg2[...] = jnp.concatenate([region[...], region[...]], axis=1)
    ch, cl = split(vel[...] - w)
    contrast = jnp.concatenate([ch, ch, cl, cl], axis=0).astype(BF16)
    label = lax.broadcasted_iota(jnp.int32, (labels, 2 * sy), 0)

    def mult_plane(x, carry):
        own = jnp.where(reg2[pl.ds(x, 1), :] == label, ab[pl.ds(x, 1), :], 0.0)
        oh, ol = split(own)
        lhs = jnp.concatenate([oh, ol, oh, ol], axis=0).astype(BF16)
        res = lax.dot_general(lhs, contrast, (((0,), (0,)), ((), ())), preferred_element_type=F32)
        mult[0, x] = res[:sy]
        mult[1, x] = res[sy:]
        return carry

    lax.fori_loop(0, sx, mult_plane, 0, unroll=8)

    @pl.when(jnp.logical_and(has_e, has_n))
    def _():
        pl.semaphore_wait(barrier, 2)

    @pl.when(jnp.logical_xor(has_e, has_n))
    def _():
        pl.semaphore_wait(barrier, 1)

    def east_copy(t, p):
        return pltpu.make_async_remote_copy(
            src_ref=east_buf.at[t, :, pl.ds(2 * p, 2)], dst_ref=west_buf.at[t, :, pl.ds(2 * p, 2)],
            send_sem=send_e.at[t, p], recv_sem=recv_w.at[t, p],
            device_id=(a + 1, b), device_id_type=MESH)

    spans = segments(sx)

    def north_copy(t, k):
        rows = pl.ds(spans[k][0] * DEPTH, (spans[k][1] - spans[k][0]) * DEPTH)
        return pltpu.make_async_remote_copy(
            src_ref=north_buf.at[t, :, rows, :], dst_ref=south_buf.at[t, :, rows, :],
            send_sem=send_n.at[t, k], recv_sem=recv_s.at[t, k],
            device_id=(a, b + 1), device_id_type=MESH)

    def spread(q, even_in, odd_in, low, high):
        whole = low == 0 and high == sx // 2

        def planes(table, values):
            if not whole:
                return halves(mm(table[2 * low * SUB:2 * high * SUB, :], values))
            out = mm(table[...], values)
            edge = 2 * DEPTH * SUB
            return jnp.concatenate([halves(out[:edge]), halves(out[edge:])], axis=0)

        even = planes(te, even_in)
        odd = planes(to, odd_in)
        res = jnp.concatenate([even + odd, even - odd], axis=0)
        size = res.shape[0]
        done = along_z(jnp.concatenate([res[:, n * sz:(n + 1) * sz] for n in range(4)], axis=0), zz[...])
        count = high - low
        for k in range(2):
            rows = pl.ds((2 * q + k) * SUB, SUB)
            for c in range(2):
                n = 2 * k + c
                block = done[n * size:(n + 1) * size].reshape(2 * count, SUB, sz)
                mid[c, low:high, rows, :] = block[:count]
                for i in range(count):
                    mid[c, sx - 1 - low - i, rows, :] = block[count + i]

    need("west_in", "south_in", "ty", "zz", "ts")
    zpad = jnp.zeros((SUB, sz), F32)
    row8 = lax.broadcasted_iota(jnp.int32, (SUB, sz), 0)

    for t in range(TICKS):
        west = west_in if t == 0 else west_buf.at[t - 1]
        south = south_in if t == 0 else south_buf.at[t - 1]
        def take_west(p):
            if t > 0:
                @pl.when(has_w)
                def _():
                    east_copy(t - 1, p).wait_recv()

            planes = []
            for j in range(2 * p, 2 * p + 2):
                plane = jnp.concatenate([west[0, j], west[1, j]], axis=1)
                planes.append(halves(mm(ty[...], right2(plane))))
            rows = [q[:, c * sz:(c + 1) * sz] for c in range(2) for q in planes]
            done = along_z(jnp.concatenate(rows, axis=0), zz[...])
            wf[:, 2 * p:2 * p + 2] = done.reshape(2, 2, sy, sz)

        def take_south(parts):
            if t > 0:
                @pl.when(has_s)
                def _():
                    for k in parts:
                        north_copy(t - 1, k).wait_recv()

            cuts = [slice(spans[k][0] * DEPTH, spans[k][1] * DEPTH) for k in parts]
            done = along_z(jnp.concatenate([south[c, rows, :] for c in range(2) for rows in cuts], axis=0), zz[...])
            size = done.shape[0] // 2
            both = jnp.concatenate([done[:size], done[size:]], axis=1)
            at = 0
            for k, rows in zip(parts, cuts):
                step = rows.stop - rows.start
                arrived[k] = both[at:at + step]
                at += step

        arrived = {}
        every = list(range(len(spans)))
        take_west(0)
        if t == 0:
            take_south(every)
            take_west(1)
        else:
            take_west(1)
            take_south(every[:2])
            for k in every[2:]:
                take_south([k])
        in_order = sorted(every, key=lambda k: spans[k][0])
        rs[...] = right2(mm(ts[...], right3(jnp.concatenate([arrived[k] for k in in_order], axis=0))))

        if t == 0:
            need("lsh", "lsl", "te", "to", "amp")

        source = t - a - b + (n_gx + n_gy - 2)
        live = jnp.where(slot[0, 0] == source, 1.0, 0.0).astype(F32)
        amps = (amp[0, source] * live, amp[1, source] * live)

        def spectrum(q):
            shared = mm(lsh[q], rs[...])
            specs = []
            for k in range(2):
                g = 2 * q + k
                rows = pl.ds(g * SUB, SUB)
                p = point[rows, :]
                parts = []
                for c in range(2):
                    wh, wl = split(wf[c, :, rows, :].reshape(DEPTH * SUB, sz))
                    ph, pw = split(p * amps[c])
                    parts.append(jnp.concatenate([wh, wl, wh, ph, pw, ph, zpad], axis=0).astype(BF16))
                rw = jnp.concatenate([rs[: sx * DEPTH, :], jnp.concatenate(parts, axis=1)], axis=0)
                lhs = jnp.concatenate([lsl[g], lw[...]], axis=1)
                coeffs = shared[k * span:(k + 1) * span] + mm(lhs, rw)
                c0, c1 = coeffs[:, :sz], coeffs[:, sz:]
                pr, qr = pq[0, g], pq[1, g]
                specs += [c0 * pr + c1 * qr, c1 * pr - c0 * qr]
            spec = jnp.concatenate(specs, axis=1)
            return right2(spec[: span // 2]), right2(spec[span // 2:])

        ahead = spectrum(0)
        for q in range(groups // 2):
            even_in, odd_in = ahead
            if q + 1 < groups // 2:
                ahead = spectrum(q + 1)
            if t + 1 == TICKS:
                spread(q, even_in, odd_in, 0, sx // 2)
            else:
                sp[2 * q] = even_in
                sp[2 * q + 1] = odd_in
                spread(q, even_in, odd_in, 0, DEPTH)

        if t + 1 == TICKS:
            break

        def one_plane(x):
            fr, fi = finish_plane(x, mid, mult, ty)
            obuf[t, 0, x] = fr.astype(BF16)
            obuf[t, 1, x] = fi.astype(BF16)
            return fr, fi

        def two_planes(i, east):
            first = one_plane(2 * i)
            second = one_plane(2 * i + 1)
            if t + 1 < TICKS:
                rows = pl.ds(pl.multiple_of(i * SUB, SUB), SUB)
                for c in range(2):
                    one = pltpu.roll(first[c][sy - SUB:], DEPTH, 0)
                    north_buf[t, c, rows, :] = jnp.where(row8 < DEPTH, one, second[c][sy - SUB:])
                    if east is not None:
                        east_buf[t, c, 2 * i - (sx - DEPTH)] = first[c]
                        east_buf[t, c, 2 * i + 1 - (sx - DEPTH)] = second[c]

        for i in range((sx - DEPTH) // 2, sx // 2):
            two_planes(i, True)

            @pl.when(has_e)
            def _():
                east_copy(t, i - (sx - DEPTH) // 2).start()

        for i in range(DEPTH // 2):
            two_planes(i, None)

        @pl.when(has_n)
        def _():
            north_copy(t, 0).start()
            north_copy(t, 1).start()

        for q in range(groups // 2):
            spread(q, sp[2 * q], sp[2 * q + 1], DEPTH, sx // 2)

        for k in range(2, len(spans)):
            for i in range(spans[k][0] // 2, spans[k][1] // 2):
                two_planes(i, None)

            @pl.when(has_n)
            def _():
                north_copy(t, k).start()

    for t in range(TICKS - 1):
        if t + 1 < TICKS:
            @pl.when(has_e)
            def _():
                for p in range(DEPTH // 2):
                    east_copy(t, p).wait_send()

            @pl.when(has_n)
            def _():
                for k in range(len(spans)):
                    north_copy(t, k).wait_send()


def solution(mesh):
    n_gx = mesh.shape["gx"]
    n_gy = mesh.shape["gy"]

    def local(west_in, south_in, region, pml_layers, vel_table, src_slot, src_cell, src_amp, wave_sq):
        sx, sy = region.shape
        sz = vel_table.shape[1]
        groups = sy // SUB
        consts = make_tables(sx, sy, sz)
        smem = pl.BlockSpec(memory_space=pltpu.SMEM)
        vmem = pl.BlockSpec(memory_space=pltpu.VMEM)
        hbm = pl.BlockSpec(memory_space=pl.ANY)
        dma = pltpu.SemaphoreType.DMA
        shape = (TICKS, 2, sx, sy, sz)
        inputs = [
            pml_layers.transpose(1, 2, 0).reshape(1, 4), src_amp, wave_sq.reshape(1, 1),
            west_in, south_in.reshape(2, sx * DEPTH, sz), region, vel_table,
            *[jnp.asarray(consts[name]) for name in NAMES],
        ]
        count = len(SCALARS)
        held = [pltpu.SMEM(v.shape, v.dtype) for v in inputs[:count]]
        held += [pltpu.VMEM(v.shape, v.dtype) for v in inputs[count:]]
        early, mid, mult = pl.pallas_call(
            functools.partial(kernel, n_gx, n_gy),
            out_shape=(
                pltpu.VMEM((TICKS - 1,) + shape[1:], BF16),
                pltpu.VMEM(shape[1:], F32),
                pltpu.VMEM(shape[1:], F32),
            ),
            in_specs=[smem] * 2 + [pl.BlockSpec(memory_space=pltpu.HBM)] * len(inputs),
            out_specs=(vmem,) * 3,
            scratch_shapes=held + [
                pltpu.VMEM((TICKS - 1, 2, DEPTH, sy, sz), F32),
                pltpu.VMEM((TICKS - 1, 2, sx * DEPTH, sz), F32),
                pltpu.VMEM((TICKS - 1, 2, DEPTH, sy, sz), F32),
                pltpu.VMEM((TICKS - 1, 2, sx * DEPTH, sz), F32),
                pltpu.VMEM(consts["lw"].shape, BF16),
                pltpu.VMEM((sy, sz), F32),
                pltpu.VMEM((2, groups, sx * SUB, sz), F32),
                pltpu.VMEM((sx, 2 * sy), jnp.int32),
                pltpu.VMEM((sx, 2 * sy), F32),
                pltpu.VMEM((2 * sx * DEPTH, 2 * sz), BF16),
                pltpu.VMEM((2, DEPTH, sy, sz), F32),
                pltpu.VMEM((groups, sx * SUB, 4 * sz), BF16),
                dma((TICKS - 1, DEPTH // 2)),
                dma((TICKS - 1, DEPTH // 2)),
                dma((TICKS - 1, INNER_PIECES + 2)),
                dma((TICKS - 1, INNER_PIECES + 2)),
                dma((len(inputs),)),
            ],
            compiler_params=pltpu.CompilerParams(
                collective_id=0, has_side_effects=True, vmem_limit_bytes=60000000),
        )(src_slot, src_cell, *inputs)
        keep = lambda v: pltpu.with_memory_space_constraint(v, pltpu.VMEM)
        return pl.pallas_call(
            finish,
            out_shape=jax.ShapeDtypeStruct(shape, BF16),
            in_specs=[vmem] * 4,
            out_specs=hbm,
            scratch_shapes=[pltpu.VMEM(shape[1:], BF16), dma((TICKS - 1 + PIECES,))],
            compiler_params=pltpu.CompilerParams(vmem_limit_bytes=16 * 1024 * 1024),
        )(keep(early), keep(mid), keep(mult), jnp.asarray(consts["ty"]))

    in_specs = (
        P(None, "gx", "gy", None),
        P(None, "gx", "gy", None),
        P("gx", "gy"),
        P(None, "gx", "gy"),
        P(),
        P("gx", "gy"),
        P("gx", "gy"),
        P(),
        P(),
    )
    out_specs = P(None, None, "gx", "gy", None)
    return jax.shard_map(local, mesh=mesh, in_specs=in_specs, out_specs=out_specs, check_vma=False)
```

```python
import functools

import jax
import jax.numpy as jnp
import numpy as np
from jax import lax
from jax.experimental import pallas as pl
from jax.experimental.pallas import tpu as pltpu
from jax.sharding import PartitionSpec as P

DEPTH = 4
TICKS = 3
PIECES = 4
SUB = 8
damping_ratio = 0.25
absorb_peak = 4.0
diagonal_base = 6.0
F32 = jnp.float32
BF16 = jnp.bfloat16
MESH = pl.DeviceIdType.MESH


def basis(count):
    k = np.arange(count, dtype=np.float64) + 1.0
    table = np.sqrt(2.0 / (count + 1.0)) * np.sin(np.pi * k[:, None] * k[None, :] / (count + 1.0))
    eigen = 2.0 - 2.0 * np.cos(np.pi * k / (count + 1.0))
    return table, eigen


def np_split(table):
    full = np.asarray(table, np.float32)
    high = full.astype(BF16)
    low = (full - high.astype(np.float32)).astype(BF16)
    return high, low


def left3(table):
    high, low = np_split(table)
    return np.concatenate([high, high, low], axis=1)


def fold(table):
    high, low = np_split(table)
    return np.concatenate([np.concatenate([high, high], 1), np.concatenate([low, np.zeros_like(low)], 1)], 0)


def split(values):
    high = values.astype(BF16).astype(F32)
    return high, values - high


def right3(values):
    high, low = split(values)
    high = high.astype(BF16)
    return jnp.concatenate([high, low.astype(BF16), high], axis=0)


def right2(values):
    high, low = split(values)
    return jnp.concatenate([high.astype(BF16), low.astype(BF16)], axis=0)


def mm(a, b):
    return jnp.dot(a, b, preferred_element_type=F32)


def halves(both):
    size = both.shape[0] // 2
    return both[:size] + both[size:]


def along_z(values, zz):
    high, low = split(values)
    both = jnp.concatenate([high.astype(BF16), low.astype(BF16)], axis=1)
    out = mm(both, zz)
    half = out.shape[1] // 2
    return out[:, :half] + out[:, half:]


def make_tables(sx, sy, sz):
    bx, ex = basis(sx)
    by, ey = basis(sy)
    bz, ez = basis(sz)
    eye = np.eye(SUB)
    groups = sy // SUB
    ls = [np_split(np.kron(np.eye(sx), by[g * SUB:(g + 1) * SUB, :DEPTH])) for g in range(groups)]
    lsh = np.stack([h for h, _ in ls])
    lsl = np.stack([low for _, low in ls])
    half = sx // 2
    order = np.concatenate([np.arange(0, sx, 2), np.arange(1, sx, 2)])
    bxo, exo = bx[order], ex[order]
    lw = left3(np.kron(bxo[:, :DEPTH], eye))
    lw = np.concatenate([lw, np.zeros((lw.shape[0], 4 * SUB), lw.dtype)], axis=1)
    even = np.kron(bx[:half, order[:half]], eye)
    odd = np.kron(bx[:half, order[half:]], eye)
    zh, zl = np_split(bz)
    zz = np.concatenate([np.concatenate([zh, zl], 1)] * 2, 0)
    return dict(
        lsh=lsh.reshape(groups // 2, -1, lsh.shape[2]),
        lsl=lsl,
        lw=lw,
        te=left3(even),
        to=left3(odd),
        tee=fold(even[:DEPTH * SUB]),
        toe=fold(odd[:DEPTH * SUB]),
        ln=np.stack([np.concatenate(np_split(np.kron(np.eye(half), by[sy - DEPTH:, g * SUB:(g + 1) * SUB])), axis=1) for g in range(groups)]),
        tn=left3(np.kron(bxo.T, np.eye(DEPTH))),
        ts=left3(np.kron(bxo, np.eye(DEPTH))),
        ty=left3(by),
        zz=zz,
        bxr=np.repeat(bxo, SUB, axis=0).astype(np.float32),
        byf=by.astype(np.float32),
        bzf=bz.astype(np.float32),
        exr=np.repeat(exo, SUB)[:, None].astype(np.float32) * np.ones((1, sz), np.float32),
        eyr=ey[:, None].astype(np.float32) * np.ones((1, sz), np.float32),
        ezr=ez[None, :].astype(np.float32),
    )


SCALARS = ("pml", "amp", "wave")
INVERSE_UNROLL = 8
NAMES = ("lsh", "lsl", "lw", "te", "to", "tee", "toe", "ln", "tn", "ts", "ty", "zz", "bxr", "byf", "bzf", "exr", "eyr", "ezr")


INPUTS = SCALARS + ("west_in", "south_in", "region", "vel") + NAMES
FIRST = ("wave", "ezr", "eyr", "exr", "bxr", "byf", "bzf", "lw", "pml", "region", "vel")
ORDER = FIRST + tuple(name for name in INPUTS if name not in FIRST)


def finish_plane(x, mid, mult, ty):
    sz = mid.shape[3]
    plane = jnp.concatenate([mid[0, x], mid[1, x]], axis=1)
    raw = mm(ty[...], right3(plane))
    re, im = raw[:, :sz], raw[:, sz:]
    mr, mi = mult[0, x], mult[1, x]
    fr = re + mr * re - mi * im
    fi = im + mr * im + mi * re
    return fr, fi


def finish(early, mid, mult, ty, out, last, sems):
    sx = mid.shape[1]
    count = early.shape[0]
    copies = [pltpu.make_async_copy(early.at[t], out.at[t], sems.at[t]) for t in range(count)]
    for copy in copies:
        copy.start()
    size = sx // PIECES
    for k in range(PIECES):
        for x in range(k * size, (k + 1) * size):
            fr, fi = finish_plane(x, mid, mult, ty)
            last[0, x] = fr.astype(BF16)
            last[1, x] = fi.astype(BF16)
        part = pl.ds(k * size, size)
        copy = pltpu.make_async_copy(last.at[:, part], out.at[count, :, part], sems.at[count + k])
        copy.start()
        copies.append(copy)
    for copy in copies:
        copy.wait()


def kernel(n_gx, n_gy, *refs):
    slot, cell = refs[:2]
    outside, (obuf, mid, mult), refs = refs[2:27], refs[27:30], refs[30:]
    inside, refs = refs[:25], refs[25:]
    pml, amp, wave = inside[:3]
    (west_in, south_in, region, vel,
     lsh, lsl, lw0, te, to, tee, toe, ln, tn, ts, ty, zz, bxr, byf, bzf, exr, eyr, ezr) = inside[3:]
    (
     west_buf, south_buf, east_buf, north_buf,
     lw, point, pq, reg2, ab, rs, wf, sp, nacc, mn,
     send_e, recv_w, send_n, recv_s, load_sem) = refs
    sx, sy = region.shape
    sz = vel.shape[1]
    labels = vel.shape[0]
    groups = sy // SUB
    span = sx * SUB
    a = lax.axis_index("gx")
    b = lax.axis_index("gy")
    has_w, has_e = a > 0, a + 1 < n_gx
    has_s, has_n = b > 0, b + 1 < n_gy

    loads = {name: pltpu.make_async_copy(src, dst, load_sem.at[i])
             for i, (name, (src, dst)) in enumerate(zip(INPUTS, zip(outside, inside)))}
    for name in ORDER:
        loads[name].start()

    def need(*names):
        for name in names:
            loads[name].wait()

    barrier = pltpu.get_barrier_semaphore()

    @pl.when(has_w)
    def _():
        pl.semaphore_signal(barrier, inc=1, device_id=(a - 1, b), device_id_type=MESH)

    @pl.when(has_s)
    def _():
        pl.semaphore_signal(barrier, inc=1, device_id=(a, b - 1), device_id_type=MESH)


    @pl.when(jnp.logical_not(has_w))
    def _():
        west_buf[...] = jnp.zeros_like(west_buf)

    @pl.when(jnp.logical_not(has_s))
    def _():
        south_buf[...] = jnp.zeros_like(south_buf)

    need("wave", "exr", "eyr", "ezr")
    w = wave[0, 0]
    damp = -damping_ratio * w

    def inverse_group(g, carry):
        y_part = eyr[pl.ds(pl.multiple_of(g * SUB, SUB), SUB), :]
        lam = exr[...].reshape(sx, SUB, sz) + y_part[None] + ezr[...][None] - w
        lam = lam.reshape(sx * SUB, sz)
        inv = 1.0 / (lam * lam + damp * damp)
        pq[0, g] = lam * inv
        pq[1, g] = damp * inv
        return carry

    lax.fori_loop(0, groups, inverse_group, 0, unroll=INVERSE_UNROLL)
    need("bxr", "byf", "bzf", "lw")

    position = cell[0, 0]
    px = position // (sy * sz)
    py = (position // sz) % sy
    pz = position % sz
    x_lane = lax.broadcasted_iota(jnp.int32, (sx * SUB, sx), 1)
    bxp = jnp.sum(jnp.where(x_lane == px, bxr[...], 0.0), axis=1, keepdims=True)
    y_lane = lax.broadcasted_iota(jnp.int32, (sy, sy), 1)
    byp = jnp.sum(jnp.where(y_lane == py, byf[...], 0.0), axis=1, keepdims=True)
    z_row = lax.broadcasted_iota(jnp.int32, (sz, sz), 0)
    bzp = jnp.sum(jnp.where(z_row == pz, bzf[...], 0.0), axis=0, keepdims=True)
    point[...] = byp * bzp
    width = lw0.shape[1]
    first = 3 * DEPTH * SUB
    lane = lax.broadcasted_iota(jnp.int32, (sx * SUB, width), 1)
    row = lax.broadcasted_iota(jnp.int32, (sx * SUB, width), 0)
    xh, xl = split(bxp)
    dyn = jnp.where(lane < first + 2 * SUB, xh, xl)
    dyn = jnp.where((lane % SUB) == (row % SUB), dyn, 0.0)
    lw[...] = jnp.where(lane < first, lw0[...].astype(F32), dyn).astype(BF16)

    xi = lax.broadcasted_iota(jnp.int32, (sx, 2 * sy), 0).astype(F32)
    lane2 = lax.broadcasted_iota(jnp.int32, (sx, 2 * sy), 1)
    yi = (lane2 % sy).astype(F32)

    need("pml", "region", "vel")

    def ramp(i, distance):
        thick = pml[0, i].astype(F32)
        portion = jnp.maximum(thick - distance, 0.0) / jnp.maximum(jnp.full_like(distance, thick), 1.0)
        return portion * portion

    def coefficients(x, y, real):
        sigma = ramp(0, x) + ramp(1, sx - 1.0 - x) + ramp(2, y) + ramp(3, sy - 1.0 - y)
        sigma = absorb_peak * sigma
        return jnp.where(real, diagonal_base, -sigma) / (diagonal_base * diagonal_base + sigma * sigma)

    ab[...] = coefficients(xi, yi, lane2 < sy)
    reg2[...] = jnp.concatenate([region[...], region[...]], axis=1)
    ch, cl = split(vel[...] - w)
    contrast = jnp.concatenate([ch, ch, cl, cl], axis=0).astype(BF16)
    label = lax.broadcasted_iota(jnp.int32, (labels, 2 * sy), 0)

    def expand(own):
        oh, ol = split(own)
        lhs = jnp.concatenate([oh, ol, oh, ol], axis=0).astype(BF16)
        return lax.dot_general(lhs, contrast, (((0,), (0,)), ((), ())), preferred_element_type=F32)

    edge = sx * DEPTH
    lane_n = lax.broadcasted_iota(jnp.int32, (labels, 2 * edge), 1)
    place = lane_n % edge
    north_ab = coefficients((place // DEPTH).astype(F32), (sy - DEPTH + place % DEPTH).astype(F32), lane_n < edge)
    y_of = sy - DEPTH + lax.broadcasted_iota(jnp.int32, (sy, 2 * edge), 1) % DEPTH
    pick = jnp.where(lax.broadcasted_iota(jnp.int32, (sy, 2 * edge), 0) == y_of, 1.0, 0.0).astype(BF16)
    spread_out = mm(region[...].astype(F32).astype(BF16), pick)
    x_of = (lax.broadcasted_iota(jnp.int32, (sx, 2 * edge), 1) % edge) // DEPTH
    own_row = lax.broadcasted_iota(jnp.int32, (sx, 2 * edge), 0) == x_of
    north_label = jnp.sum(jnp.where(own_row, spread_out, 0.0), axis=0, keepdims=True)
    north_mult = expand(jnp.where(north_label == lax.broadcasted_iota(jnp.int32, (labels, 2 * edge), 0).astype(F32), north_ab, 0.0))
    mn[0] = north_mult[:edge]
    mn[1] = north_mult[edge:]

    def mult_plane(x, carry):
        res = expand(jnp.where(reg2[pl.ds(x, 1), :] == label, ab[pl.ds(x, 1), :], 0.0))
        mult[0, x] = res[:sy]
        mult[1, x] = res[sy:]
        return carry

    for x in list(range(DEPTH)) + list(range(sx - DEPTH, sx)):
        mult_plane(x, 0)

    @pl.when(jnp.logical_and(has_e, has_n))
    def _():
        pl.semaphore_wait(barrier, 2)

    @pl.when(jnp.logical_xor(has_e, has_n))
    def _():
        pl.semaphore_wait(barrier, 1)

    def east_copy(t, p):
        return pltpu.make_async_remote_copy(
            src_ref=east_buf.at[t, :, pl.ds(2 * p, 2)], dst_ref=west_buf.at[t, :, pl.ds(2 * p, 2)],
            send_sem=send_e.at[t, p], recv_sem=recv_w.at[t, p],
            device_id=(a + 1, b), device_id_type=MESH)

    def north_copy(t):
        return pltpu.make_async_remote_copy(
            src_ref=north_buf.at[t], dst_ref=south_buf.at[t],
            send_sem=send_n.at[t], recv_sem=recv_s.at[t],
            device_id=(a, b + 1), device_id_type=MESH)

    def spread(q, even_in, odd_in, low, high):
        if high == DEPTH:
            cut = 2 * DEPTH * SUB
            outs = []
            for table, values, side in ((tee, even_in, 0), (toe, odd_in, 1)):
                total = None
                ends = []
                for k in range(2):
                    high_part, low_part = ln[2 * q + k, :, :span // 2], ln[2 * q + k, :, span // 2:]
                    lhs = jnp.concatenate([
                        table[...],
                        jnp.concatenate([high_part, high_part], axis=1),
                        jnp.concatenate([low_part, jnp.zeros_like(low_part)], axis=1)], axis=0)
                    out = mm(lhs, values[:, 2 * k * sz:2 * (k + 1) * sz])
                    ends.append(halves(out[:cut]))
                    part = halves(out[cut:])
                    total = part if total is None else total + part
                rows = pl.ds(side * edge // 2, edge // 2)
                nacc[rows, :] = total if q == 0 else nacc[rows, :] + total
                outs.append(jnp.concatenate(ends, axis=1))
            even, odd = outs
        else:
            rows = slice(low * SUB, high * SUB)
            even = mm(te[rows, :], jnp.concatenate([even_in, even_in[:span // 2]], axis=0))
            odd = mm(to[rows, :], jnp.concatenate([odd_in, odd_in[:span // 2]], axis=0))
        res = jnp.concatenate([even + odd, even - odd], axis=0)
        size = res.shape[0]
        done = along_z(jnp.concatenate([res[:, n * sz:(n + 1) * sz] for n in range(4)], axis=0), zz[...])
        count = high - low
        for k in range(2):
            rows = pl.ds((2 * q + k) * SUB, SUB)
            for c in range(2):
                n = 2 * k + c
                block = done[n * size:(n + 1) * size].reshape(2 * count, SUB, sz)
                mid[c, low:high, rows, :] = block[:count]
                for i in range(count):
                    mid[c, sx - 1 - low - i, rows, :] = block[count + i]

    need("west_in", "south_in", "ty", "zz", "ts")
    zpad = jnp.zeros((SUB, sz), F32)

    for t in range(TICKS):
        west = west_in if t == 0 else west_buf.at[t - 1]
        south = south_in if t == 0 else south_buf.at[t - 1]
        def take_west():
            if t > 0:
                @pl.when(has_w)
                def _():
                    for p in range(DEPTH // 2):
                        east_copy(t - 1, p).wait_recv()

            planes = []
            for j in range(DEPTH):
                plane = jnp.concatenate([west[0, j], west[1, j]], axis=1)
                planes.append(mm(ty[...], right3(plane)))
            rows = [q[:, c * sz:(c + 1) * sz] for c in range(2) for q in planes]
            done = along_z(jnp.concatenate(rows, axis=0), zz[...])
            wf[...] = done.reshape(2, DEPTH, sy, sz)

        if t > 0:
            @pl.when(has_s)
            def _():
                north_copy(t - 1).wait_recv()

        done = along_z(jnp.concatenate([south[0], south[1]], axis=0), zz[...])
        done = jnp.concatenate([done[:edge], done[edge:]], axis=1)
        rs[...] = right2(mm(ts[...], right3(done)))
        take_west()

        if t == 0:
            need("lsh", "lsl", "te", "to", "tee", "toe", "ln", "tn", "amp")

        source = t - a - b + (n_gx + n_gy - 2)
        live = jnp.where(slot[0, 0] == source, 1.0, 0.0).astype(F32)
        amps = (amp[0, source] * live, amp[1, source] * live)

        def spectrum(q):
            shared = mm(jnp.concatenate([lsh[q], lsh[q]], axis=1), rs[...])
            specs = []
            for k in range(2):
                g = 2 * q + k
                rows = pl.ds(g * SUB, SUB)
                p = point[rows, :]
                parts = []
                for c in range(2):
                    wh, wl = split(wf[c, :, rows, :].reshape(DEPTH * SUB, sz))
                    ph, pw = split(p * amps[c])
                    parts.append(jnp.concatenate([wh, wl, wh, ph, pw, ph, zpad], axis=0).astype(BF16))
                rw = jnp.concatenate([rs[: sx * DEPTH, :], jnp.concatenate(parts, axis=1)], axis=0)
                coeffs = shared[k * span:(k + 1) * span] + mm(jnp.concatenate([lsl[g], lw[...]], axis=1), rw)
                c0, c1 = coeffs[:, :sz], coeffs[:, sz:]
                pr, qr = pq[0, g], pq[1, g]
                specs += [c0 * pr + c1 * qr, c1 * pr - c0 * qr]
            spec = jnp.concatenate(specs, axis=1)
            return right2(spec[: span // 2]), right2(spec[span // 2:])

        ahead = spectrum(0)
        for q in range(groups // 2):
            even_in, odd_in = ahead
            if q + 1 < groups // 2:
                ahead = spectrum(q + 1)
            if t + 1 == TICKS:
                spread(q, even_in, odd_in, 0, sx // 2)
            else:
                sp[2 * q] = even_in
                sp[2 * q + 1] = odd_in
                spread(q, even_in, odd_in, 0, DEPTH)

        if t + 1 == TICKS:
            break

        def one_plane(x):
            fr, fi = finish_plane(x, mid, mult, ty)
            obuf[t, 0, x] = fr.astype(BF16)
            obuf[t, 1, x] = fi.astype(BF16)
            return fr, fi

        def east_planes(p):
            for j in range(2 * p, 2 * p + 2):
                field = one_plane(sx - DEPTH + j)
                for c in range(2):
                    east_buf[t, c, j] = field[c]

            @pl.when(has_e)
            def _():
                east_copy(t, p).start()

        back = mm(tn[...], right3(nacc[...]))
        back = along_z(jnp.concatenate([back[:, :sz], back[:, sz:]], axis=0), zz[...])
        east_planes(0)
        re, im = back[:edge], back[edge:]
        north_buf[t, 0] = re + mn[0] * re - mn[1] * im
        north_buf[t, 1] = im + mn[0] * im + mn[1] * re
        east_planes(1)

        @pl.when(has_n)
        def _():
            north_copy(t).start()

        if t == 0:
            lax.fori_loop(DEPTH, sx - DEPTH, mult_plane, 0, unroll=8)

        for q in range(groups // 2):
            spread(q, sp[2 * q], sp[2 * q + 1], DEPTH, sx // 2)

        for x in range(sx - DEPTH):
            one_plane(x)

    for t in range(TICKS - 1):
        if t + 1 < TICKS:
            @pl.when(has_e)
            def _():
                for p in range(DEPTH // 2):
                    east_copy(t, p).wait_send()

            @pl.when(has_n)
            def _():
                north_copy(t).wait_send()


def solution(mesh):
    n_gx = mesh.shape["gx"]
    n_gy = mesh.shape["gy"]

    def local(west_in, south_in, region, pml_layers, vel_table, src_slot, src_cell, src_amp, wave_sq):
        sx, sy = region.shape
        sz = vel_table.shape[1]
        groups = sy // SUB
        consts = make_tables(sx, sy, sz)
        smem = pl.BlockSpec(memory_space=pltpu.SMEM)
        vmem = pl.BlockSpec(memory_space=pltpu.VMEM)
        hbm = pl.BlockSpec(memory_space=pl.ANY)
        dma = pltpu.SemaphoreType.DMA
        shape = (TICKS, 2, sx, sy, sz)
        inputs = [
            pml_layers.transpose(1, 2, 0).reshape(1, 4), src_amp, wave_sq.reshape(1, 1),
            west_in, south_in.reshape(2, sx * DEPTH, sz), region, vel_table,
            *[jnp.asarray(consts[name]) for name in NAMES],
        ]
        count = len(SCALARS)
        held = [pltpu.SMEM(v.shape, v.dtype) for v in inputs[:count]]
        held += [pltpu.VMEM(v.shape, v.dtype) for v in inputs[count:]]
        early, mid, mult = pl.pallas_call(
            functools.partial(kernel, n_gx, n_gy),
            out_shape=(
                pltpu.VMEM((TICKS - 1,) + shape[1:], BF16),
                pltpu.VMEM(shape[1:], F32),
                pltpu.VMEM(shape[1:], F32),
            ),
            in_specs=[smem] * 2 + [pl.BlockSpec(memory_space=pltpu.HBM)] * len(inputs),
            out_specs=(vmem,) * 3,
            scratch_shapes=held + [
                pltpu.VMEM((TICKS - 1, 2, DEPTH, sy, sz), F32),
                pltpu.VMEM((TICKS - 1, 2, sx * DEPTH, sz), F32),
                pltpu.VMEM((TICKS - 1, 2, DEPTH, sy, sz), F32),
                pltpu.VMEM((TICKS - 1, 2, sx * DEPTH, sz), F32),
                pltpu.VMEM(consts["lw"].shape, BF16),
                pltpu.VMEM((sy, sz), F32),
                pltpu.VMEM((2, groups, sx * SUB, sz), F32),
                pltpu.VMEM((sx, 2 * sy), jnp.int32),
                pltpu.VMEM((sx, 2 * sy), F32),
                pltpu.VMEM((2 * sx * DEPTH, 2 * sz), BF16),
                pltpu.VMEM((2, DEPTH, sy, sz), F32),
                pltpu.VMEM((groups, sx * SUB, 4 * sz), BF16),
                pltpu.VMEM((sx * DEPTH, 2 * sz), F32),
                pltpu.VMEM((2, sx * DEPTH, sz), F32),
                dma((TICKS - 1, DEPTH // 2)),
                dma((TICKS - 1, DEPTH // 2)),
                dma((TICKS - 1,)),
                dma((TICKS - 1,)),
                dma((len(inputs),)),
            ],
            compiler_params=pltpu.CompilerParams(
                collective_id=0, has_side_effects=True, vmem_limit_bytes=60000000),
        )(src_slot, src_cell, *inputs)
        keep = lambda v: pltpu.with_memory_space_constraint(v, pltpu.VMEM)
        return pl.pallas_call(
            finish,
            out_shape=jax.ShapeDtypeStruct(shape, BF16),
            in_specs=[vmem] * 4,
            out_specs=hbm,
            scratch_shapes=[pltpu.VMEM(shape[1:], BF16), dma((TICKS - 1 + PIECES,))],
            compiler_params=pltpu.CompilerParams(vmem_limit_bytes=16 * 1024 * 1024),
        )(keep(early), keep(mid), keep(mult), jnp.asarray(consts["ty"]))

    in_specs = (
        P(None, "gx", "gy", None),
        P(None, "gx", "gy", None),
        P("gx", "gy"),
        P(None, "gx", "gy"),
        P(),
        P("gx", "gy"),
        P("gx", "gy"),
        P(),
        P(),
    )
    out_specs = P(None, None, "gx", "gy", None)
    return jax.shard_map(local, mesh=mesh, in_specs=in_specs, out_specs=out_specs, check_vma=False)
```

```python
import functools

import jax
import jax.numpy as jnp
import numpy as np
from jax import lax
from jax.experimental import pallas as pl
from jax.experimental.pallas import tpu as pltpu
from jax.sharding import PartitionSpec as P

DEPTH = 4
TICKS = 3
PIECES = 8
SUB = 8
damping_ratio = 0.25
absorb_peak = 4.0
diagonal_base = 6.0
F32 = jnp.float32
BF16 = jnp.bfloat16
MESH = pl.DeviceIdType.MESH


def basis(count):
    k = np.arange(count, dtype=np.float64) + 1.0
    table = np.sqrt(2.0 / (count + 1.0)) * np.sin(np.pi * k[:, None] * k[None, :] / (count + 1.0))
    eigen = 2.0 - 2.0 * np.cos(np.pi * k / (count + 1.0))
    return table, eigen


def np_split(table):
    full = np.asarray(table, np.float32)
    high = full.astype(BF16)
    low = (full - high.astype(np.float32)).astype(BF16)
    return high, low


def left3(table):
    high, low = np_split(table)
    return np.concatenate([high, high, low], axis=1)


def fold(table):
    high, low = np_split(table)
    return np.concatenate([np.concatenate([high, high], 1), np.concatenate([low, np.zeros_like(low)], 1)], 0)


def split(values):
    high = values.astype(BF16).astype(F32)
    return high, values - high


def right3(values):
    high, low = split(values)
    high = high.astype(BF16)
    return jnp.concatenate([high, low.astype(BF16), high], axis=0)


def right2(values):
    high, low = split(values)
    return jnp.concatenate([high.astype(BF16), low.astype(BF16)], axis=0)


def mm(a, b):
    return jnp.dot(a, b, preferred_element_type=F32)


def halves(both):
    size = both.shape[0] // 2
    return both[:size] + both[size:]


def along_z(values, zz):
    high, low = split(values)
    both = jnp.concatenate([high.astype(BF16), low.astype(BF16)], axis=1)
    out = mm(both, zz)
    half = out.shape[1] // 2
    return out[:, :half] + out[:, half:]


def make_tables(sx, sy, sz):
    bx, ex = basis(sx)
    by, ey = basis(sy)
    bz, ez = basis(sz)
    eye = np.eye(SUB)
    groups = sy // SUB
    ls = [np_split(np.kron(np.eye(sx), by[g * SUB:(g + 1) * SUB, :DEPTH])) for g in range(groups)]
    lsh = np.stack([h for h, _ in ls])
    lsl = np.stack([low for _, low in ls])
    half = sx // 2
    order = np.concatenate([np.arange(0, sx, 2), np.arange(1, sx, 2)])
    bxo, exo = bx[order], ex[order]
    lw = left3(np.kron(bxo[:, :DEPTH], eye))
    lw = np.concatenate([lw, np.zeros((lw.shape[0], 4 * SUB), lw.dtype)], axis=1)
    even = np.kron(bx[:half, order[:half]], eye)
    odd = np.kron(bx[:half, order[half:]], eye)
    zh, zl = np_split(bz)
    zz = np.concatenate([np.concatenate([zh, zl], 1)] * 2, 0)
    return dict(
        lsh=lsh.reshape(groups // 2, -1, lsh.shape[2]),
        lsl=lsl,
        lw=lw,
        te=left3(even),
        to=left3(odd),
        tee=fold(even[:DEPTH * SUB]),
        toe=fold(odd[:DEPTH * SUB]),
        ln=np.stack([np.concatenate(np_split(np.kron(np.eye(half), by[sy - DEPTH:, g * SUB:(g + 1) * SUB])), axis=1) for g in range(groups)]),
        tn=left3(np.kron(bxo.T, np.eye(DEPTH))),
        ts=left3(np.kron(bxo, np.eye(DEPTH))),
        ty=left3(by),
        zz=zz,
        bxr=np.repeat(bxo, SUB, axis=0).astype(np.float32),
        byf=by.astype(np.float32),
        bzf=bz.astype(np.float32),
        exr=np.repeat(exo, SUB)[:, None].astype(np.float32) * np.ones((1, sz), np.float32),
        eyr=ey[:, None].astype(np.float32) * np.ones((1, sz), np.float32),
        ezr=ez[None, :].astype(np.float32),
    )


SCALARS = ("pml", "amp", "wave")
INVERSE_UNROLL = 8
NAMES = ("lsh", "lsl", "lw", "te", "to", "tee", "toe", "ln", "tn", "ts", "ty", "zz", "bxr", "byf", "bzf", "exr", "eyr", "ezr")


INPUTS = SCALARS + ("west_in", "south_in", "region", "vel") + NAMES
FIRST = ("wave", "ezr", "eyr", "exr", "bxr", "byf", "bzf", "lw", "pml", "region", "vel", "west_in", "south_in", "ty", "zz", "ts")
ORDER = FIRST + tuple(name for name in INPUTS if name not in FIRST)


def finish_plane(x, mid, mult, ty):
    sz = mid.shape[3]
    plane = jnp.concatenate([mid[0, x], mid[1, x]], axis=1)
    raw = mm(ty[...], right3(plane))
    re, im = raw[:, :sz], raw[:, sz:]
    mr, mi = mult[0, x], mult[1, x]
    fr = mr * re - mi * im
    fi = mr * im + mi * re
    return fr, fi


def finish(early, mid, mult, ty, out, last, sems):
    sx = mid.shape[1]
    count = early.shape[0]
    copies = [pltpu.make_async_copy(early.at[t], out.at[t], sems.at[t]) for t in range(count)]
    for copy in copies:
        copy.start()
    size = sx // PIECES
    for k in range(PIECES):
        for x in range(k * size, (k + 1) * size):
            fr, fi = finish_plane(x, mid, mult, ty)
            last[0, x] = fr.astype(BF16)
            last[1, x] = fi.astype(BF16)
        part = pl.ds(k * size, size)
        copy = pltpu.make_async_copy(last.at[:, part], out.at[count, :, part], sems.at[count + k])
        copy.start()
        copies.append(copy)
    for copy in copies:
        copy.wait()


def kernel(n_gx, n_gy, *refs):
    slot, cell = refs[:2]
    outside, (obuf, mid, mult), refs = refs[2:27], refs[27:30], refs[30:]
    inside, refs = refs[:25], refs[25:]
    pml, amp, wave = inside[:3]
    (west_in, south_in, region, vel,
     lsh, lsl, lw0, te, to, tee, toe, ln, tn, ts, ty, zz, bxr, byf, bzf, exr, eyr, ezr) = inside[3:]
    (
     west_buf, south_buf, east_buf, north_buf,
     lw, point, pq, reg2, ab, rs, wf, sp, nacc, mn,
     send_e, recv_w, send_n, recv_s, load_sem) = refs
    sx, sy = region.shape
    sz = vel.shape[1]
    labels = vel.shape[0]
    groups = sy // SUB
    span = sx * SUB
    a = lax.axis_index("gx")
    b = lax.axis_index("gy")
    has_w, has_e = a > 0, a + 1 < n_gx
    has_s, has_n = b > 0, b + 1 < n_gy

    loads = {name: pltpu.make_async_copy(src, dst, load_sem.at[i])
             for i, (name, (src, dst)) in enumerate(zip(INPUTS, zip(outside, inside)))}
    for name in ORDER:
        loads[name].start()

    def need(*names):
        for name in names:
            loads[name].wait()

    barrier = pltpu.get_barrier_semaphore()

    @pl.when(has_w)
    def _():
        pl.semaphore_signal(barrier, inc=1, device_id=(a - 1, b), device_id_type=MESH)

    @pl.when(has_s)
    def _():
        pl.semaphore_signal(barrier, inc=1, device_id=(a, b - 1), device_id_type=MESH)


    @pl.when(jnp.logical_not(has_w))
    def _():
        west_buf[...] = jnp.zeros_like(west_buf)

    @pl.when(jnp.logical_not(has_s))
    def _():
        south_buf[...] = jnp.zeros_like(south_buf)

    need("wave", "exr", "eyr", "ezr", "bxr", "byf", "bzf", "lw", "pml", "region", "vel", "west_in", "south_in", "ty", "zz", "ts")
    w = wave[0, 0]
    damp = -damping_ratio * w

    def inverse_group(g, carry):
        y_part = eyr[pl.ds(pl.multiple_of(g * SUB, SUB), SUB), :]
        lam = exr[...].reshape(sx, SUB, sz) + y_part[None] + ezr[...][None] - w
        lam = lam.reshape(sx * SUB, sz)
        inv = 1.0 / (lam * lam + damp * damp)
        pq[0, g] = lam * inv
        pq[1, g] = damp * inv
        return carry

    lax.fori_loop(0, groups, inverse_group, 0, unroll=INVERSE_UNROLL)

    position = cell[0, 0]
    px = position // (sy * sz)
    py = (position // sz) % sy
    pz = position % sz
    x_lane = lax.broadcasted_iota(jnp.int32, (sx * SUB, sx), 1)
    bxp = jnp.sum(jnp.where(x_lane == px, bxr[...], 0.0), axis=1, keepdims=True)
    y_lane = lax.broadcasted_iota(jnp.int32, (sy, sy), 1)
    byp = jnp.sum(jnp.where(y_lane == py, byf[...], 0.0), axis=1, keepdims=True)
    z_row = lax.broadcasted_iota(jnp.int32, (sz, sz), 0)
    bzp = jnp.sum(jnp.where(z_row == pz, bzf[...], 0.0), axis=0, keepdims=True)
    point[...] = byp * bzp
    width = lw0.shape[1]
    first = 3 * DEPTH * SUB
    lane = lax.broadcasted_iota(jnp.int32, (sx * SUB, width), 1)
    row = lax.broadcasted_iota(jnp.int32, (sx * SUB, width), 0)
    xh, xl = split(bxp)
    dyn = jnp.where(lane < first + 2 * SUB, xh, xl)
    dyn = jnp.where((lane % SUB) == (row % SUB), dyn, 0.0)
    lw[...] = jnp.where(lane < first, lw0[...].astype(F32), dyn).astype(BF16)

    xi = lax.broadcasted_iota(jnp.int32, (sx, 2 * sy), 0).astype(F32)
    lane2 = lax.broadcasted_iota(jnp.int32, (sx, 2 * sy), 1)
    yi = (lane2 % sy).astype(F32)

    def ramp(i, distance):
        thick = pml[0, i].astype(F32)
        portion = jnp.maximum(thick - distance, 0.0) / jnp.maximum(jnp.full_like(distance, thick), 1.0)
        return portion * portion

    def coefficients(x, y, real):
        sigma = ramp(0, x) + ramp(1, sx - 1.0 - x) + ramp(2, y) + ramp(3, sy - 1.0 - y)
        sigma = absorb_peak * sigma
        return jnp.where(real, diagonal_base, -sigma) / (diagonal_base * diagonal_base + sigma * sigma)

    ab[...] = coefficients(xi, yi, lane2 < sy)
    reg2[...] = jnp.concatenate([region[...], region[...]], axis=1)
    ch, cl = split(vel[...] - w)
    contrast = jnp.concatenate([ch, ch, cl, cl], axis=0).astype(BF16)
    label = lax.broadcasted_iota(jnp.int32, (labels, 2 * sy), 0)

    def expand(own):
        oh, ol = split(own)
        lhs = jnp.concatenate([oh, ol, oh, ol], axis=0).astype(BF16)
        return lax.dot_general(lhs, contrast, (((0,), (0,)), ((), ())), preferred_element_type=F32)

    edge = sx * DEPTH
    lane_n = lax.broadcasted_iota(jnp.int32, (labels, 2 * edge), 1)
    place = lane_n % edge
    north_ab = coefficients((place // DEPTH).astype(F32), (sy - DEPTH + place % DEPTH).astype(F32), lane_n < edge)
    y_of = sy - DEPTH + lax.broadcasted_iota(jnp.int32, (sy, 2 * edge), 1) % DEPTH
    pick = jnp.where(lax.broadcasted_iota(jnp.int32, (sy, 2 * edge), 0) == y_of, 1.0, 0.0).astype(BF16)
    spread_out = mm(region[...].astype(F32).astype(BF16), pick)
    x_of = (lax.broadcasted_iota(jnp.int32, (sx, 2 * edge), 1) % edge) // DEPTH
    own_row = lax.broadcasted_iota(jnp.int32, (sx, 2 * edge), 0) == x_of
    north_label = jnp.sum(jnp.where(own_row, spread_out, 0.0), axis=0, keepdims=True)
    north_mult = expand(jnp.where(north_label == lax.broadcasted_iota(jnp.int32, (labels, 2 * edge), 0).astype(F32), north_ab, 0.0))
    mn[0] = 1.0 + north_mult[:edge]
    mn[1] = north_mult[edge:]

    def mult_plane(x, carry):
        res = expand(jnp.where(reg2[pl.ds(x, 1), :] == label, ab[pl.ds(x, 1), :], 0.0))
        mult[0, x] = 1.0 + res[:sy]
        mult[1, x] = res[sy:]
        return carry

    for x in list(range(DEPTH)) + list(range(sx - DEPTH, sx)):
        mult_plane(x, 0)

    def east_copy(t, p):
        return pltpu.make_async_remote_copy(
            src_ref=east_buf.at[t, :, pl.ds(2 * p, 2)], dst_ref=west_buf.at[t, :, pl.ds(2 * p, 2)],
            send_sem=send_e.at[t, p], recv_sem=recv_w.at[t, p],
            device_id=(a + 1, b), device_id_type=MESH)

    def north_copy(t):
        return pltpu.make_async_remote_copy(
            src_ref=north_buf.at[t], dst_ref=south_buf.at[t],
            send_sem=send_n.at[t], recv_sem=recv_s.at[t],
            device_id=(a, b + 1), device_id_type=MESH)

    def spread(q, even_in, odd_in, low, high):
        if high == DEPTH:
            cut = 2 * DEPTH * SUB
            outs = []
            for table, values, side in ((tee, even_in, 0), (toe, odd_in, 1)):
                total = None
                ends = []
                for k in range(2):
                    high_part, low_part = ln[2 * q + k, :, :span // 2], ln[2 * q + k, :, span // 2:]
                    lhs = jnp.concatenate([
                        table[...],
                        jnp.concatenate([high_part, high_part], axis=1),
                        jnp.concatenate([low_part, jnp.zeros_like(low_part)], axis=1)], axis=0)
                    out = mm(lhs, values[:, 2 * k * sz:2 * (k + 1) * sz])
                    ends.append(halves(out[:cut]))
                    part = halves(out[cut:])
                    total = part if total is None else total + part
                rows = pl.ds(side * edge // 2, edge // 2)
                nacc[rows, :] = total if q == 0 else nacc[rows, :] + total
                outs.append(jnp.concatenate(ends, axis=1))
            even, odd = outs
        else:
            rows = slice(low * SUB, high * SUB)
            even = mm(te[rows, :], jnp.concatenate([even_in, even_in[:span // 2]], axis=0))
            odd = mm(to[rows, :], jnp.concatenate([odd_in, odd_in[:span // 2]], axis=0))
        res = jnp.concatenate([even + odd, even - odd], axis=0)
        size = res.shape[0]
        done = along_z(jnp.concatenate([res[:, n * sz:(n + 1) * sz] for n in range(4)], axis=0), zz[...])
        count = high - low
        for k in range(2):
            rows = pl.ds((2 * q + k) * SUB, SUB)
            for c in range(2):
                n = 2 * k + c
                block = done[n * size:(n + 1) * size].reshape(2 * count, SUB, sz)
                mid[c, low:high, rows, :] = block[:count]
                for i in range(count):
                    mid[c, sx - 1 - low - i, rows, :] = block[count + i]

    zpad = jnp.zeros((SUB, sz), F32)

    for t in range(TICKS):
        west = west_in if t == 0 else west_buf.at[t - 1]
        south = south_in if t == 0 else south_buf.at[t - 1]
        def take_west():
            if t > 0:
                @pl.when(has_w)
                def _():
                    for p in range(DEPTH // 2):
                        east_copy(t - 1, p).wait_recv()

            planes = []
            for j in range(DEPTH):
                plane = jnp.concatenate([west[0, j], west[1, j]], axis=1)
                planes.append(mm(ty[...], right3(plane)))
            rows = [q[:, c * sz:(c + 1) * sz] for c in range(2) for q in planes]
            done = along_z(jnp.concatenate(rows, axis=0), zz[...])
            wf[...] = done.reshape(2, DEPTH, sy, sz)

        if t > 0:
            @pl.when(has_s)
            def _():
                north_copy(t - 1).wait_recv()

        done = along_z(jnp.concatenate([south[0], south[1]], axis=0), zz[...])
        done = jnp.concatenate([done[:edge], done[edge:]], axis=1)
        rs[...] = right2(mm(ts[...], right3(done)))
        take_west()

        if t == 0:
            need("lsh", "lsl", "te", "to", "tee", "toe", "ln", "tn", "amp")

        source = t - a - b + (n_gx + n_gy - 2)
        live = jnp.where(slot[0, 0] == source, 1.0, 0.0).astype(F32)
        amps = (amp[0, source] * live, amp[1, source] * live)

        def spectrum(q):
            shared = mm(jnp.concatenate([lsh[q], lsh[q]], axis=1), rs[...])
            specs = []
            for k in range(2):
                g = 2 * q + k
                rows = pl.ds(g * SUB, SUB)
                p = point[rows, :]
                parts = []
                for c in range(2):
                    wh, wl = split(wf[c, :, rows, :].reshape(DEPTH * SUB, sz))
                    ph, pw = split(p * amps[c])
                    parts.append(jnp.concatenate([wh, wl, wh, ph, pw, ph, zpad], axis=0).astype(BF16))
                rw = jnp.concatenate([rs[: sx * DEPTH, :], jnp.concatenate(parts, axis=1)], axis=0)
                coeffs = shared[k * span:(k + 1) * span] + mm(jnp.concatenate([lsl[g], lw[...]], axis=1), rw)
                c0, c1 = coeffs[:, :sz], coeffs[:, sz:]
                pr, qr = pq[0, g], pq[1, g]
                specs += [c0 * pr + c1 * qr, c1 * pr - c0 * qr]
            spec = jnp.concatenate(specs, axis=1)
            return right2(spec[: span // 2]), right2(spec[span // 2:])

        if t + 1 == TICKS:
            ahead = spectrum(0)
            for q in range(groups // 2):
                even_in, odd_in = ahead
                if q + 1 < groups // 2:
                    ahead = spectrum(q + 1)
                spread(q, even_in, odd_in, 0, sx // 2)
            break

        for q in range(groups // 2):
            sp[2 * q], sp[2 * q + 1] = spectrum(q)
        for q in range(groups // 2):
            spread(q, sp[2 * q], sp[2 * q + 1], 0, DEPTH)


        def one_plane(x):
            fr, fi = finish_plane(x, mid, mult, ty)
            obuf[t, 0, x] = fr.astype(BF16)
            obuf[t, 1, x] = fi.astype(BF16)
            return fr, fi

        def east_planes(p):
            for j in range(2 * p, 2 * p + 2):
                field = one_plane(sx - DEPTH + j)
                for c in range(2):
                    east_buf[t, c, j] = field[c]

            @pl.when(has_e)
            def _():
                east_copy(t, p).start()

        if t == 0:
            @pl.when(jnp.logical_and(has_e, has_n))
            def _():
                pl.semaphore_wait(barrier, 2)

            @pl.when(jnp.logical_xor(has_e, has_n))
            def _():
                pl.semaphore_wait(barrier, 1)

        back = mm(tn[...], right3(nacc[...]))
        back = along_z(jnp.concatenate([back[:, :sz], back[:, sz:]], axis=0), zz[...])
        east_planes(0)
        re, im = back[:edge], back[edge:]
        north_buf[t, 0] = mn[0] * re - mn[1] * im
        north_buf[t, 1] = mn[0] * im + mn[1] * re
        east_planes(1)

        @pl.when(has_n)
        def _():
            north_copy(t).start()

        if t == 0:
            lax.fori_loop(DEPTH, sx - DEPTH, mult_plane, 0, unroll=8)

        for q in range(groups // 2):
            spread(q, sp[2 * q], sp[2 * q + 1], DEPTH, sx // 2)

        for x in range(sx - DEPTH):
            one_plane(x)

    for t in range(TICKS - 1):
        if t + 1 < TICKS:
            @pl.when(has_e)
            def _():
                for p in range(DEPTH // 2):
                    east_copy(t, p).wait_send()

            @pl.when(has_n)
            def _():
                north_copy(t).wait_send()


def solution(mesh):
    n_gx = mesh.shape["gx"]
    n_gy = mesh.shape["gy"]

    def local(west_in, south_in, region, pml_layers, vel_table, src_slot, src_cell, src_amp, wave_sq):
        sx, sy = region.shape
        sz = vel_table.shape[1]
        groups = sy // SUB
        consts = make_tables(sx, sy, sz)
        smem = pl.BlockSpec(memory_space=pltpu.SMEM)
        vmem = pl.BlockSpec(memory_space=pltpu.VMEM)
        hbm = pl.BlockSpec(memory_space=pl.ANY)
        dma = pltpu.SemaphoreType.DMA
        shape = (TICKS, 2, sx, sy, sz)
        inputs = [
            pml_layers.transpose(1, 2, 0).reshape(1, 4), src_amp, wave_sq.reshape(1, 1),
            west_in, south_in.reshape(2, sx * DEPTH, sz), region, vel_table,
            *[jnp.asarray(consts[name]) for name in NAMES],
        ]
        count = len(SCALARS)
        held = [pltpu.SMEM(v.shape, v.dtype) for v in inputs[:count]]
        held += [pltpu.VMEM(v.shape, v.dtype) for v in inputs[count:]]
        early, mid, mult = pl.pallas_call(
            functools.partial(kernel, n_gx, n_gy),
            out_shape=(
                pltpu.VMEM((TICKS - 1,) + shape[1:], BF16),
                pltpu.VMEM(shape[1:], F32),
                pltpu.VMEM(shape[1:], F32),
            ),
            in_specs=[smem] * 2 + [pl.BlockSpec(memory_space=pltpu.HBM)] * len(inputs),
            out_specs=(vmem,) * 3,
            scratch_shapes=held + [
                pltpu.VMEM((TICKS - 1, 2, DEPTH, sy, sz), F32),
                pltpu.VMEM((TICKS - 1, 2, sx * DEPTH, sz), F32),
                pltpu.VMEM((TICKS - 1, 2, DEPTH, sy, sz), F32),
                pltpu.VMEM((TICKS - 1, 2, sx * DEPTH, sz), F32),
                pltpu.VMEM(consts["lw"].shape, BF16),
                pltpu.VMEM((sy, sz), F32),
                pltpu.VMEM((2, groups, sx * SUB, sz), F32),
                pltpu.VMEM((sx, 2 * sy), jnp.int32),
                pltpu.VMEM((sx, 2 * sy), F32),
                pltpu.VMEM((2 * sx * DEPTH, 2 * sz), BF16),
                pltpu.VMEM((2, DEPTH, sy, sz), F32),
                pltpu.VMEM((groups, sx * SUB, 4 * sz), BF16),
                pltpu.VMEM((sx * DEPTH, 2 * sz), F32),
                pltpu.VMEM((2, sx * DEPTH, sz), F32),
                dma((TICKS - 1, DEPTH // 2)),
                dma((TICKS - 1, DEPTH // 2)),
                dma((TICKS - 1,)),
                dma((TICKS - 1,)),
                dma((len(inputs),)),
            ],
            compiler_params=pltpu.CompilerParams(
                collective_id=0, has_side_effects=True, vmem_limit_bytes=60000000),
        )(src_slot, src_cell, *inputs)
        keep = lambda v: pltpu.with_memory_space_constraint(v, pltpu.VMEM)
        return pl.pallas_call(
            finish,
            out_shape=jax.ShapeDtypeStruct(shape, BF16),
            in_specs=[vmem] * 4,
            out_specs=hbm,
            scratch_shapes=[pltpu.VMEM(shape[1:], BF16), dma((TICKS - 1 + PIECES,))],
            compiler_params=pltpu.CompilerParams(vmem_limit_bytes=16 * 1024 * 1024),
        )(keep(early), keep(mid), keep(mult), jnp.asarray(consts["ty"]))

    in_specs = (
        P(None, "gx", "gy", None),
        P(None, "gx", "gy", None),
        P("gx", "gy"),
        P(None, "gx", "gy"),
        P(),
        P("gx", "gy"),
        P("gx", "gy"),
        P(),
        P(),
    )
    out_specs = P(None, None, "gx", "gy", None)
    return jax.shard_map(local, mesh=mesh, in_specs=in_specs, out_specs=out_specs, check_vma=False)
```

```python
import functools

import jax
import jax.numpy as jnp
import numpy as np
from jax import lax
from jax.experimental import pallas as pl
from jax.experimental.pallas import tpu as pltpu
from jax.sharding import PartitionSpec as P

DEPTH = 4
TICKS = 3
PIECES = 4
SUB = 8
damping_ratio = 0.25
absorb_peak = 4.0
diagonal_base = 6.0
F32 = jnp.float32
BF16 = jnp.bfloat16
MESH = pl.DeviceIdType.MESH


def basis(count):
    k = np.arange(count, dtype=np.float64) + 1.0
    table = np.sqrt(2.0 / (count + 1.0)) * np.sin(np.pi * k[:, None] * k[None, :] / (count + 1.0))
    eigen = 2.0 - 2.0 * np.cos(np.pi * k / (count + 1.0))
    return table, eigen


def np_split(table):
    full = np.asarray(table, np.float32)
    high = full.astype(BF16)
    low = (full - high.astype(np.float32)).astype(BF16)
    return high, low


def left3(table):
    high, low = np_split(table)
    return np.concatenate([high, high, low], axis=1)


def fold(table):
    high, low = np_split(table)
    return np.concatenate([np.concatenate([high, high], 1), np.concatenate([low, np.zeros_like(low)], 1)], 0)


def split(values):
    high = values.astype(BF16).astype(F32)
    return high, values - high


def right3(values):
    high, low = split(values)
    high = high.astype(BF16)
    return jnp.concatenate([high, low.astype(BF16), high], axis=0)


def right2(values):
    high, low = split(values)
    return jnp.concatenate([high.astype(BF16), low.astype(BF16)], axis=0)


def mm(a, b):
    return jnp.dot(a, b, preferred_element_type=F32)


def halves(both):
    size = both.shape[0] // 2
    return both[:size] + both[size:]


def along_z(values, zz):
    high, low = split(values)
    both = jnp.concatenate([high.astype(BF16), low.astype(BF16)], axis=1)
    out = mm(both, zz)
    half = out.shape[1] // 2
    return out[:, :half] + out[:, half:]


def make_tables(sx, sy, sz):
    bx, ex = basis(sx)
    by, ey = basis(sy)
    bz, ez = basis(sz)
    eye = np.eye(SUB)
    groups = sy // SUB
    ls = [np_split(np.kron(np.eye(sx), by[g * SUB:(g + 1) * SUB, :DEPTH])) for g in range(groups)]
    lsh = np.stack([h for h, _ in ls])
    lsl = np.stack([low for _, low in ls])
    half = sx // 2
    order = np.concatenate([np.arange(0, sx, 2), np.arange(1, sx, 2)])
    bxo, exo = bx[order], ex[order]
    lw = left3(np.kron(bxo[:, :DEPTH], eye))
    lw = np.concatenate([lw, np.zeros((lw.shape[0], 4 * SUB), lw.dtype)], axis=1)
    even = np.kron(bx[:half, order[:half]], eye)
    odd = np.kron(bx[:half, order[half:]], eye)
    zh, zl = np_split(bz)
    zz = np.concatenate([np.concatenate([zh, zl], 1)] * 2, 0)
    return dict(
        lsh=lsh.reshape(groups // 2, -1, lsh.shape[2]),
        lsl=lsl,
        lw=lw,
        te=left3(even),
        to=left3(odd),
        tee=fold(even[:DEPTH * SUB]),
        toe=fold(odd[:DEPTH * SUB]),
        ln=np.stack([np.concatenate(np_split(np.kron(np.eye(half), by[sy - DEPTH:, g * SUB:(g + 1) * SUB])), axis=1) for g in range(groups)]),
        tn=left3(np.kron(bxo.T, np.eye(DEPTH))),
        ts=left3(np.kron(bxo, np.eye(DEPTH))),
        ty=left3(by),
        zz=zz,
        bxr=np.repeat(bxo, SUB, axis=0).astype(np.float32),
        byf=by.astype(np.float32),
        bzf=bz.astype(np.float32),
        exr=np.repeat(exo, SUB)[:, None].astype(np.float32) * np.ones((1, sz), np.float32),
        eyr=ey[:, None].astype(np.float32) * np.ones((1, sz), np.float32),
        ezr=ez[None, :].astype(np.float32),
    )


SCALARS = ("pml", "amp", "wave")
INVERSE_UNROLL = 8
NAMES = ("lsh", "lsl", "lw", "te", "to", "tee", "toe", "ln", "tn", "ts", "ty", "zz", "bxr", "byf", "bzf", "exr", "eyr", "ezr")


INPUTS = SCALARS + ("west_in", "south_in", "region", "vel") + NAMES
FIRST = ("wave", "ezr", "eyr", "exr", "bxr", "byf", "bzf", "lw", "pml", "region", "vel", "west_in", "south_in", "ty", "zz", "ts")
ORDER = FIRST + tuple(name for name in INPUTS if name not in FIRST)


def finish_plane(x, mid, mult, ty):
    sz = mid.shape[3]
    plane = jnp.concatenate([mid[0, x], mid[1, x]], axis=1)
    raw = mm(ty[...], right3(plane))
    re, im = raw[:, :sz], raw[:, sz:]
    mr, mi = mult[0, x], mult[1, x]
    fr = mr * re - mi * im
    fi = mr * im + mi * re
    return fr, fi


def finish(early, mid, mult, ty, out, last, sems):
    sx = mid.shape[1]
    count = early.shape[0]
    copies = [pltpu.make_async_copy(early, out.at[pl.ds(0, count)], sems.at[0])]
    for copy in copies:
        copy.start()
    size = sx // PIECES
    for k in range(PIECES):
        for x in range(k * size, (k + 1) * size):
            fr, fi = finish_plane(x, mid, mult, ty)
            last[0, x] = fr.astype(BF16)
            last[1, x] = fi.astype(BF16)
        part = pl.ds(k * size, size)
        copy = pltpu.make_async_copy(last.at[:, part], out.at[count, :, part], sems.at[count + k])
        copy.start()
        copies.append(copy)
    for copy in copies:
        copy.wait()


def kernel(n_gx, n_gy, *refs):
    slot, cell = refs[:2]
    outside, (obuf, mid, mult), refs = refs[2:27], refs[27:30], refs[30:]
    inside, refs = refs[:25], refs[25:]
    pml, amp, wave = inside[:3]
    (west_in, south_in, region, vel,
     lsh, lsl, lw0, te, to, tee, toe, ln, tn, ts, ty, zz, bxr, byf, bzf, exr, eyr, ezr) = inside[3:]
    (
     west_buf, south_buf, east_buf, north_buf,
     lw, point, pq, reg2, ab, rs, wf, sp, nacc, mn, west_side,
     send_e, recv_w, send_n, recv_s, load_sem) = refs
    sx, sy = region.shape
    sz = vel.shape[1]
    labels = vel.shape[0]
    groups = sy // SUB
    span = sx * SUB
    a = lax.axis_index("gx")
    b = lax.axis_index("gy")
    has_w, has_e = a > 0, a + 1 < n_gx
    has_s, has_n = b > 0, b + 1 < n_gy

    loads = {name: pltpu.make_async_copy(src, dst, load_sem.at[i])
             for i, (name, (src, dst)) in enumerate(zip(INPUTS, zip(outside, inside)))}
    for name in ORDER:
        loads[name].start()

    def need(*names):
        for name in names:
            loads[name].wait()

    barrier = pltpu.get_barrier_semaphore()

    @pl.when(has_w)
    def _():
        pl.semaphore_signal(barrier, inc=1, device_id=(a - 1, b), device_id_type=MESH)

    @pl.when(has_s)
    def _():
        pl.semaphore_signal(barrier, inc=1, device_id=(a, b - 1), device_id_type=MESH)


    @pl.when(jnp.logical_not(has_w))
    def _():
        west_buf[...] = jnp.zeros_like(west_buf)

    @pl.when(jnp.logical_not(has_s))
    def _():
        south_buf[...] = jnp.zeros_like(south_buf)

    need("wave", "exr", "eyr", "ezr", "bxr", "byf", "bzf", "lw", "pml", "region", "vel", "west_in", "south_in", "ty", "zz", "ts")
    w = wave[0, 0]
    damp = -damping_ratio * w

    def inverse_group(g, carry):
        y_part = eyr[pl.ds(pl.multiple_of(g * SUB, SUB), SUB), :]
        lam = exr[...].reshape(sx, SUB, sz) + y_part[None] + ezr[...][None] - w
        lam = lam.reshape(sx * SUB, sz)
        inv = 1.0 / (lam * lam + damp * damp)
        pq[0, g] = lam * inv
        pq[1, g] = damp * inv
        return carry

    lax.fori_loop(0, groups, inverse_group, 0, unroll=INVERSE_UNROLL)

    position = cell[0, 0]
    px = position // (sy * sz)
    py = (position // sz) % sy
    pz = position % sz
    x_lane = lax.broadcasted_iota(jnp.int32, (sx * SUB, sx), 1)
    bxp = jnp.sum(jnp.where(x_lane == px, bxr[...], 0.0), axis=1, keepdims=True)
    y_lane = lax.broadcasted_iota(jnp.int32, (sy, sy), 1)
    byp = jnp.sum(jnp.where(y_lane == py, byf[...], 0.0), axis=1, keepdims=True)
    z_row = lax.broadcasted_iota(jnp.int32, (sz, sz), 0)
    bzp = jnp.sum(jnp.where(z_row == pz, bzf[...], 0.0), axis=0, keepdims=True)
    point[...] = byp * bzp
    width = lw0.shape[1]
    first = 3 * DEPTH * SUB
    lane = lax.broadcasted_iota(jnp.int32, (sx * SUB, width), 1)
    row = lax.broadcasted_iota(jnp.int32, (sx * SUB, width), 0)
    xh, xl = split(bxp)
    dyn = jnp.where(lane < first + 2 * SUB, xh, xl)
    dyn = jnp.where((lane % SUB) == (row % SUB), dyn, 0.0)
    lw[...] = jnp.where(lane < first, lw0[...].astype(F32), dyn).astype(BF16)

    xi = lax.broadcasted_iota(jnp.int32, (sx, 2 * sy), 0).astype(F32)
    lane2 = lax.broadcasted_iota(jnp.int32, (sx, 2 * sy), 1)
    yi = (lane2 % sy).astype(F32)

    def ramp(i, distance):
        thick = pml[0, i].astype(F32)
        portion = jnp.maximum(thick - distance, 0.0) / jnp.maximum(jnp.full_like(distance, thick), 1.0)
        return portion * portion

    def coefficients(x, y, real):
        sigma = ramp(0, x) + ramp(1, sx - 1.0 - x) + ramp(2, y) + ramp(3, sy - 1.0 - y)
        sigma = absorb_peak * sigma
        return jnp.where(real, diagonal_base, -sigma) / (diagonal_base * diagonal_base + sigma * sigma)

    ab[...] = coefficients(xi, yi, lane2 < sy)
    reg2[...] = jnp.concatenate([region[...], region[...]], axis=1)
    ch, cl = split(vel[...] - w)
    contrast = jnp.concatenate([ch, ch, cl, cl], axis=0).astype(BF16)
    label = lax.broadcasted_iota(jnp.int32, (labels, 2 * sy), 0)

    def expand(own):
        oh, ol = split(own)
        lhs = jnp.concatenate([oh, ol, oh, ol], axis=0).astype(BF16)
        return lax.dot_general(lhs, contrast, (((0,), (0,)), ((), ())), preferred_element_type=F32)

    edge = sx * DEPTH
    lane_n = lax.broadcasted_iota(jnp.int32, (labels, 2 * edge), 1)
    place = lane_n % edge
    north_ab = coefficients((place // DEPTH).astype(F32), (sy - DEPTH + place % DEPTH).astype(F32), lane_n < edge)
    y_of = sy - DEPTH + lax.broadcasted_iota(jnp.int32, (sy, 2 * edge), 1) % DEPTH
    pick = jnp.where(lax.broadcasted_iota(jnp.int32, (sy, 2 * edge), 0) == y_of, 1.0, 0.0).astype(BF16)
    spread_out = mm(region[...].astype(F32).astype(BF16), pick)
    x_of = (lax.broadcasted_iota(jnp.int32, (sx, 2 * edge), 1) % edge) // DEPTH
    own_row = lax.broadcasted_iota(jnp.int32, (sx, 2 * edge), 0) == x_of
    north_label = jnp.sum(jnp.where(own_row, spread_out, 0.0), axis=0, keepdims=True)
    north_mult = expand(jnp.where(north_label == lax.broadcasted_iota(jnp.int32, (labels, 2 * edge), 0).astype(F32), north_ab, 0.0))
    mn[0] = 1.0 + north_mult[:edge]
    mn[1] = north_mult[edge:]

    def mult_plane(x, carry):
        res = expand(jnp.where(reg2[pl.ds(x, 1), :] == label, ab[pl.ds(x, 1), :], 0.0))
        mult[0, x] = 1.0 + res[:sy]
        mult[1, x] = res[sy:]
        return carry

    for x in list(range(DEPTH)) + list(range(sx - DEPTH, sx)):
        mult_plane(x, 0)

    def east_copy(t, p):
        return pltpu.make_async_remote_copy(
            src_ref=east_buf.at[t, :, pl.ds(2 * p, 2)], dst_ref=west_buf.at[t, :, pl.ds(2 * p, 2)],
            send_sem=send_e.at[t, p], recv_sem=recv_w.at[t, p],
            device_id=(a + 1, b), device_id_type=MESH)

    def north_copy(t):
        return pltpu.make_async_remote_copy(
            src_ref=north_buf.at[t], dst_ref=south_buf.at[t],
            send_sem=send_n.at[t], recv_sem=recv_s.at[t],
            device_id=(a, b + 1), device_id_type=MESH)

    def spread(q, even_in, odd_in, low, high):
        if high == DEPTH:
            cut = 2 * DEPTH * SUB
            outs = []
            for table, values, side in ((tee, even_in, 0), (toe, odd_in, 1)):
                total = None
                ends = []
                for k in range(2):
                    high_part, low_part = ln[2 * q + k, :, :span // 2], ln[2 * q + k, :, span // 2:]
                    lhs = jnp.concatenate([
                        table[...],
                        jnp.concatenate([high_part, high_part], axis=1),
                        jnp.concatenate([low_part, jnp.zeros_like(low_part)], axis=1)], axis=0)
                    out = mm(lhs, values[:, 2 * k * sz:2 * (k + 1) * sz])
                    ends.append(halves(out[:cut]))
                    part = halves(out[cut:])
                    total = part if total is None else total + part
                rows = pl.ds(side * edge // 2, edge // 2)
                nacc[rows, :] = total if q == 0 else nacc[rows, :] + total
                outs.append(jnp.concatenate(ends, axis=1))
            even, odd = outs
        else:
            rows = slice(low * SUB, high * SUB)
            even = mm(te[rows, :], jnp.concatenate([even_in, even_in[:span // 2]], axis=0))
            odd = mm(to[rows, :], jnp.concatenate([odd_in, odd_in[:span // 2]], axis=0))
        mirror = list(range(sx - 1 - low, sx - 1 - high, -1))
        if high == DEPTH:
            west_side[q] = even + odd
            res = even - odd
            held = mirror
        elif low == DEPTH:
            res = jnp.concatenate([west_side[q], even + odd, even - odd], axis=0)
            held = list(range(high)) + mirror
        else:
            res = jnp.concatenate([even + odd, even - odd], axis=0)
            held = list(range(high)) + mirror
        size = res.shape[0]
        done = along_z(jnp.concatenate([res[:, n * sz:(n + 1) * sz] for n in range(4)], axis=0), zz[...])
        for k in range(2):
            rows = pl.ds((2 * q + k) * SUB, SUB)
            for c in range(2):
                n = 2 * k + c
                block = done[n * size:(n + 1) * size].reshape(len(held), SUB, sz)
                for i, x in enumerate(held):
                    mid[c, x, rows, :] = block[i]

    zpad = jnp.zeros((SUB, sz), F32)

    for t in range(TICKS):
        west = west_in if t == 0 else west_buf.at[t - 1]
        south = south_in if t == 0 else south_buf.at[t - 1]
        def take_west():
            planes = []
            for j in range(DEPTH):
                plane = jnp.concatenate([west[0, j], west[1, j]], axis=1)
                planes.append(mm(ty[...], right3(plane)))
            rows = [q[:, c * sz:(c + 1) * sz] for c in range(2) for q in planes]
            done = along_z(jnp.concatenate(rows, axis=0), zz[...])
            wf[...] = done.reshape(2, DEPTH, sy, sz)

        if t > 0:
            @pl.when(has_s)
            def _():
                north_copy(t - 1).wait_recv()

            @pl.when(has_w)
            def _():
                for p in range(DEPTH // 2):
                    east_copy(t - 1, p).wait_recv()

        done = along_z(jnp.concatenate([south[0], south[1]], axis=0), zz[...])
        done = jnp.concatenate([done[:edge], done[edge:]], axis=1)
        rs[...] = right2(mm(ts[...], right3(done)))
        take_west()

        if t == 0:
            need("lsh", "lsl", "te", "to", "tee", "toe", "ln", "tn", "amp")

        source = t - a - b + (n_gx + n_gy - 2)
        live = jnp.where(slot[0, 0] == source, 1.0, 0.0).astype(F32)
        amps = (amp[0, source] * live, amp[1, source] * live)

        def spectrum(q):
            shared = mm(jnp.concatenate([lsh[q], lsh[q]], axis=1), rs[...])
            specs = []
            for k in range(2):
                g = 2 * q + k
                rows = pl.ds(g * SUB, SUB)
                p = point[rows, :]
                parts = []
                for c in range(2):
                    wh, wl = split(wf[c, :, rows, :].reshape(DEPTH * SUB, sz))
                    ph, pw = split(p * amps[c])
                    parts.append(jnp.concatenate([wh, wl, wh, ph, pw, ph, zpad], axis=0).astype(BF16))
                rw = jnp.concatenate([rs[: sx * DEPTH, :], jnp.concatenate(parts, axis=1)], axis=0)
                coeffs = shared[k * span:(k + 1) * span] + mm(jnp.concatenate([lsl[g], lw[...]], axis=1), rw)
                c0, c1 = coeffs[:, :sz], coeffs[:, sz:]
                pr, qr = pq[0, g], pq[1, g]
                specs += [c0 * pr + c1 * qr, c1 * pr - c0 * qr]
            spec = jnp.concatenate(specs, axis=1)
            return right2(spec[: span // 2]), right2(spec[span // 2:])

        if t + 1 == TICKS:
            ahead = spectrum(0)
            for q in range(groups // 2):
                even_in, odd_in = ahead
                if q + 1 < groups // 2:
                    ahead = spectrum(q + 1)
                spread(q, even_in, odd_in, 0, sx // 2)
            break

        for q in range(groups // 2):
            sp[2 * q], sp[2 * q + 1] = spectrum(q)
        for q in range(groups // 2):
            spread(q, sp[2 * q], sp[2 * q + 1], 0, DEPTH)


        def one_plane(x):
            fr, fi = finish_plane(x, mid, mult, ty)
            obuf[t, 0, x] = fr.astype(BF16)
            obuf[t, 1, x] = fi.astype(BF16)
            return fr, fi

        def east_planes(p):
            for j in range(2 * p, 2 * p + 2):
                field = one_plane(sx - DEPTH + j)
                for c in range(2):
                    east_buf[t, c, j] = field[c]

            @pl.when(has_e)
            def _():
                east_copy(t, p).start()

        if t == 0:
            @pl.when(jnp.logical_and(has_e, has_n))
            def _():
                pl.semaphore_wait(barrier, 2)

            @pl.when(jnp.logical_xor(has_e, has_n))
            def _():
                pl.semaphore_wait(barrier, 1)

        east_planes(0)
        back = mm(tn[...], right3(nacc[...]))
        back = along_z(jnp.concatenate([back[:, :sz], back[:, sz:]], axis=0), zz[...])
        re, im = back[:edge], back[edge:]
        north_buf[t, 0] = mn[0] * re - mn[1] * im
        north_buf[t, 1] = mn[0] * im + mn[1] * re
        east_planes(1)

        @pl.when(has_n)
        def _():
            north_copy(t).start()

        if t == 0:
            lax.fori_loop(DEPTH, sx - DEPTH, mult_plane, 0, unroll=8)

        for q in range(groups // 2):
            spread(q, sp[2 * q], sp[2 * q + 1], DEPTH, sx // 2)

        for x in range(sx - DEPTH):
            one_plane(x)

    for t in range(TICKS - 1):
        if t + 1 < TICKS:
            @pl.when(has_e)
            def _():
                for p in range(DEPTH // 2):
                    east_copy(t, p).wait_send()

            @pl.when(has_n)
            def _():
                north_copy(t).wait_send()


def solution(mesh):
    n_gx = mesh.shape["gx"]
    n_gy = mesh.shape["gy"]

    def local(west_in, south_in, region, pml_layers, vel_table, src_slot, src_cell, src_amp, wave_sq):
        sx, sy = region.shape
        sz = vel_table.shape[1]
        groups = sy // SUB
        consts = make_tables(sx, sy, sz)
        smem = pl.BlockSpec(memory_space=pltpu.SMEM)
        vmem = pl.BlockSpec(memory_space=pltpu.VMEM)
        hbm = pl.BlockSpec(memory_space=pl.ANY)
        dma = pltpu.SemaphoreType.DMA
        shape = (TICKS, 2, sx, sy, sz)
        inputs = [
            pml_layers.transpose(1, 2, 0).reshape(1, 4), src_amp, wave_sq.reshape(1, 1),
            west_in, south_in.reshape(2, sx * DEPTH, sz), region, vel_table,
            *[jnp.asarray(consts[name]) for name in NAMES],
        ]
        count = len(SCALARS)
        held = [pltpu.SMEM(v.shape, v.dtype) for v in inputs[:count]]
        held += [pltpu.VMEM(v.shape, v.dtype) for v in inputs[count:]]
        early, mid, mult = pl.pallas_call(
            functools.partial(kernel, n_gx, n_gy),
            out_shape=(
                pltpu.VMEM((TICKS - 1,) + shape[1:], BF16),
                pltpu.VMEM(shape[1:], F32),
                pltpu.VMEM(shape[1:], F32),
            ),
            in_specs=[smem] * 2 + [pl.BlockSpec(memory_space=pltpu.HBM)] * len(inputs),
            out_specs=(vmem,) * 3,
            scratch_shapes=held + [
                pltpu.VMEM((TICKS - 1, 2, DEPTH, sy, sz), F32),
                pltpu.VMEM((TICKS - 1, 2, sx * DEPTH, sz), F32),
                pltpu.VMEM((TICKS - 1, 2, DEPTH, sy, sz), F32),
                pltpu.VMEM((TICKS - 1, 2, sx * DEPTH, sz), F32),
                pltpu.VMEM(consts["lw"].shape, BF16),
                pltpu.VMEM((sy, sz), F32),
                pltpu.VMEM((2, groups, sx * SUB, sz), F32),
                pltpu.VMEM((sx, 2 * sy), jnp.int32),
                pltpu.VMEM((sx, 2 * sy), F32),
                pltpu.VMEM((2 * sx * DEPTH, 2 * sz), BF16),
                pltpu.VMEM((2, DEPTH, sy, sz), F32),
                pltpu.VMEM((groups, sx * SUB, 4 * sz), BF16),
                pltpu.VMEM((sx * DEPTH, 2 * sz), F32),
                pltpu.VMEM((2, sx * DEPTH, sz), F32),
                pltpu.VMEM((groups // 2, DEPTH * SUB, 4 * sz), F32),
                dma((TICKS - 1, DEPTH // 2)),
                dma((TICKS - 1, DEPTH // 2)),
                dma((TICKS - 1,)),
                dma((TICKS - 1,)),
                dma((len(inputs),)),
            ],
            compiler_params=pltpu.CompilerParams(
                collective_id=0, has_side_effects=True, vmem_limit_bytes=60000000),
        )(src_slot, src_cell, *inputs)
        keep = lambda v: pltpu.with_memory_space_constraint(v, pltpu.VMEM)
        return pl.pallas_call(
            finish,
            out_shape=jax.ShapeDtypeStruct(shape, BF16),
            in_specs=[vmem] * 4,
            out_specs=hbm,
            scratch_shapes=[pltpu.VMEM(shape[1:], BF16), dma((TICKS - 1 + PIECES,))],
            compiler_params=pltpu.CompilerParams(vmem_limit_bytes=16 * 1024 * 1024),
        )(keep(early), keep(mid), keep(mult), jnp.asarray(consts["ty"]))

    in_specs = (
        P(None, "gx", "gy", None),
        P(None, "gx", "gy", None),
        P("gx", "gy"),
        P(None, "gx", "gy"),
        P(),
        P("gx", "gy"),
        P("gx", "gy"),
        P(),
        P(),
    )
    out_specs = P(None, None, "gx", "gy", None)
    return jax.shard_map(local, mesh=mesh, in_specs=in_specs, out_specs=out_specs, check_vma=False)
```

```python
import functools

import jax
import jax.numpy as jnp
import numpy as np
from jax import lax
from jax.experimental import pallas as pl
from jax.experimental.pallas import tpu as pltpu
from jax.sharding import PartitionSpec as P

DEPTH = 4
TICKS = 3
PIECES = 4
SUB = 8
damping_ratio = 0.25
absorb_peak = 4.0
diagonal_base = 6.0
F32 = jnp.float32
BF16 = jnp.bfloat16
MESH = pl.DeviceIdType.MESH


def basis(count):
    k = np.arange(count, dtype=np.float64) + 1.0
    table = np.sqrt(2.0 / (count + 1.0)) * np.sin(np.pi * k[:, None] * k[None, :] / (count + 1.0))
    eigen = 2.0 - 2.0 * np.cos(np.pi * k / (count + 1.0))
    return table, eigen


def np_split(table):
    full = np.asarray(table, np.float32)
    high = full.astype(BF16)
    low = (full - high.astype(np.float32)).astype(BF16)
    return high, low


def left3(table):
    high, low = np_split(table)
    return np.concatenate([high, high, low], axis=1)


def fold(table):
    high, low = np_split(table)
    return np.concatenate([np.concatenate([high, high], 1), np.concatenate([low, np.zeros_like(low)], 1)], 0)


def split(values):
    high = values.astype(BF16).astype(F32)
    return high, values - high


def right3(values):
    high, low = split(values)
    high = high.astype(BF16)
    return jnp.concatenate([high, low.astype(BF16), high], axis=0)


def right2(values):
    high, low = split(values)
    return jnp.concatenate([high.astype(BF16), low.astype(BF16)], axis=0)


def mm(a, b):
    return jnp.dot(a, b, preferred_element_type=F32)


def halves(both):
    size = both.shape[0] // 2
    return both[:size] + both[size:]


def along_z(values, zz):
    high, low = split(values)
    both = jnp.concatenate([high.astype(BF16), low.astype(BF16)], axis=1)
    out = mm(both, zz)
    half = out.shape[1] // 2
    return out[:, :half] + out[:, half:]


def make_tables(sx, sy, sz):
    bx, ex = basis(sx)
    by, ey = basis(sy)
    bz, ez = basis(sz)
    eye = np.eye(SUB)
    groups = sy // SUB
    ls = [np_split(np.kron(np.eye(sx), by[g * SUB:(g + 1) * SUB, :DEPTH])) for g in range(groups)]
    lsh = np.stack([h for h, _ in ls])
    lsl = np.stack([low for _, low in ls])
    half = sx // 2
    order = np.concatenate([np.arange(0, sx, 2), np.arange(1, sx, 2)])
    bxo, exo = bx[order], ex[order]
    lw = left3(np.kron(bxo[:, :DEPTH], eye))
    lw = np.concatenate([lw, np.zeros((lw.shape[0], 4 * SUB), lw.dtype)], axis=1)
    even = np.kron(bx[:half, order[:half]], eye)
    odd = np.kron(bx[:half, order[half:]], eye)
    zh, zl = np_split(bz)
    zz = np.concatenate([np.concatenate([zh, zl], 1)] * 2, 0)
    return dict(
        lsh=lsh.reshape(groups // 2, -1, lsh.shape[2]),
        lsl=lsl,
        lw=lw,
        te=left3(even),
        to=left3(odd),
        tee=fold(even[:DEPTH * SUB]),
        toe=fold(odd[:DEPTH * SUB]),
        ln=np.stack([np.concatenate(np_split(np.kron(np.eye(half), by[sy - DEPTH:, g * SUB:(g + 1) * SUB])), axis=1) for g in range(groups)]),
        tn=left3(np.kron(bxo.T, np.eye(DEPTH))),
        ts=left3(np.kron(bxo, np.eye(DEPTH))),
        ty=left3(by),
        zz=zz,
        bxr=np.repeat(bxo, SUB, axis=0).astype(np.float32),
        byf=by.astype(np.float32),
        bzf=bz.astype(np.float32),
        exr=np.repeat(exo, SUB)[:, None].astype(np.float32) * np.ones((1, sz), np.float32),
        eyr=ey[:, None].astype(np.float32) * np.ones((1, sz), np.float32),
        ezr=ez[None, :].astype(np.float32),
    )


SCALARS = ("pml", "amp", "wave")
INVERSE_UNROLL = 8
NAMES = ("lsh", "lsl", "lw", "te", "to", "tee", "toe", "ln", "tn", "ts", "ty", "zz", "bxr", "byf", "bzf", "exr", "eyr", "ezr")


INPUTS = SCALARS + ("west_in", "south_in", "region", "vel") + NAMES
FIRST = ("wave", "ezr", "eyr", "exr", "bxr", "byf", "bzf", "lw", "pml", "region", "vel", "west_in", "south_in", "ty", "zz", "ts")
ORDER = FIRST + tuple(name for name in INPUTS if name not in FIRST)


def finish_plane(x, mid, mult, ty):
    sz = mid.shape[3]
    plane = jnp.concatenate([mid[0, x], mid[1, x]], axis=1)
    raw = mm(ty[...], right3(plane))
    re, im = raw[:, :sz], raw[:, sz:]
    mr, mi = mult[0, x], mult[1, x]
    fr = mr * re - mi * im
    fi = mr * im + mi * re
    return fr, fi


def finish(early, mid, mult, ty, out, last, sems):
    sx = mid.shape[1]
    count = early.shape[0]
    copies = [pltpu.make_async_copy(early, out.at[pl.ds(0, count)], sems.at[0])]
    for copy in copies:
        copy.start()
    size = sx // PIECES
    for k in range(PIECES):
        for x in range(k * size, (k + 1) * size):
            fr, fi = finish_plane(x, mid, mult, ty)
            last[0, x] = fr.astype(BF16)
            last[1, x] = fi.astype(BF16)
        part = pl.ds(k * size, size)
        copy = pltpu.make_async_copy(last.at[:, part], out.at[count, :, part], sems.at[count + k])
        copy.start()
        copies.append(copy)
    for copy in copies:
        copy.wait()


def kernel(n_gx, n_gy, *refs):
    slot, cell = refs[:2]
    outside, (obuf, mid, mult), refs = refs[2:27], refs[27:30], refs[30:]
    inside, refs = refs[:25], refs[25:]
    pml, amp, wave = inside[:3]
    (west_in, south_in, region, vel,
     lsh, lsl, lw0, te, to, tee, toe, ln, tn, ts, ty, zz, bxr, byf, bzf, exr, eyr, ezr) = inside[3:]
    (
     west_buf, south_buf, east_buf, north_buf,
     lw, point, pq, reg2, ab, rs, wf, sp, nacc, mn, west_side,
     send_e, recv_w, send_n, recv_s, load_sem) = refs
    sx, sy = region.shape
    sz = vel.shape[1]
    labels = vel.shape[0]
    groups = sy // SUB
    span = sx * SUB
    a = lax.axis_index("gx")
    b = lax.axis_index("gy")
    has_w, has_e = a > 0, a + 1 < n_gx
    has_s, has_n = b > 0, b + 1 < n_gy

    loads = {name: pltpu.make_async_copy(src, dst, load_sem.at[i])
             for i, (name, (src, dst)) in enumerate(zip(INPUTS, zip(outside, inside)))}
    for name in ORDER:
        loads[name].start()

    def need(*names):
        for name in names:
            loads[name].wait()

    barrier = pltpu.get_barrier_semaphore()

    @pl.when(has_w)
    def _():
        pl.semaphore_signal(barrier, inc=1, device_id=(a - 1, b), device_id_type=MESH)

    @pl.when(has_s)
    def _():
        pl.semaphore_signal(barrier, inc=1, device_id=(a, b - 1), device_id_type=MESH)


    @pl.when(jnp.logical_not(has_w))
    def _():
        west_buf[...] = jnp.zeros_like(west_buf)

    @pl.when(jnp.logical_not(has_s))
    def _():
        south_buf[...] = jnp.zeros_like(south_buf)

    need("wave", "exr", "eyr", "ezr", "bxr", "byf", "bzf", "lw", "pml", "region", "vel", "west_in", "south_in", "ty", "zz", "ts")
    w = wave[0, 0]
    damp = -damping_ratio * w

    def inverse_group(g, carry):
        y_part = eyr[pl.ds(pl.multiple_of(g * SUB, SUB), SUB), :]
        lam = exr[...].reshape(sx, SUB, sz) + y_part[None] + ezr[...][None] - w
        lam = lam.reshape(sx * SUB, sz)
        inv = 1.0 / (lam * lam + damp * damp)
        pq[0, g] = lam * inv
        pq[1, g] = damp * inv
        return carry

    lax.fori_loop(0, groups, inverse_group, 0, unroll=INVERSE_UNROLL)

    position = cell[0, 0]
    px = position // (sy * sz)
    py = (position // sz) % sy
    pz = position % sz
    x_lane = lax.broadcasted_iota(jnp.int32, (sx * SUB, sx), 1)
    bxp = jnp.sum(jnp.where(x_lane == px, bxr[...], 0.0), axis=1, keepdims=True)
    y_lane = lax.broadcasted_iota(jnp.int32, (sy, sy), 1)
    byp = jnp.sum(jnp.where(y_lane == py, byf[...], 0.0), axis=1, keepdims=True)
    z_row = lax.broadcasted_iota(jnp.int32, (sz, sz), 0)
    bzp = jnp.sum(jnp.where(z_row == pz, bzf[...], 0.0), axis=0, keepdims=True)
    point[...] = byp * bzp
    width = lw0.shape[1]
    first = 3 * DEPTH * SUB
    lane = lax.broadcasted_iota(jnp.int32, (sx * SUB, width), 1)
    row = lax.broadcasted_iota(jnp.int32, (sx * SUB, width), 0)
    xh, xl = split(bxp)
    dyn = jnp.where(lane < first + 2 * SUB, xh, xl)
    dyn = jnp.where((lane % SUB) == (row % SUB), dyn, 0.0)
    lw[...] = jnp.where(lane < first, lw0[...].astype(F32), dyn).astype(BF16)

    xi = lax.broadcasted_iota(jnp.int32, (sx, 2 * sy), 0).astype(F32)
    lane2 = lax.broadcasted_iota(jnp.int32, (sx, 2 * sy), 1)
    yi = (lane2 % sy).astype(F32)

    def ramp(i, distance):
        thick = pml[0, i].astype(F32)
        portion = jnp.maximum(thick - distance, 0.0) / jnp.maximum(jnp.full_like(distance, thick), 1.0)
        return portion * portion

    def coefficients(x, y, real):
        sigma = ramp(0, x) + ramp(1, sx - 1.0 - x) + ramp(2, y) + ramp(3, sy - 1.0 - y)
        sigma = absorb_peak * sigma
        return jnp.where(real, diagonal_base, -sigma) / (diagonal_base * diagonal_base + sigma * sigma)

    ab[...] = coefficients(xi, yi, lane2 < sy)
    reg2[...] = jnp.concatenate([region[...], region[...]], axis=1)
    ch, cl = split(vel[...] - w)
    contrast = jnp.concatenate([ch, ch, cl, cl], axis=0).astype(BF16)
    label = lax.broadcasted_iota(jnp.int32, (labels, 2 * sy), 0)

    def expand(own):
        oh, ol = split(own)
        lhs = jnp.concatenate([oh, ol, oh, ol], axis=0).astype(BF16)
        return lax.dot_general(lhs, contrast, (((0,), (0,)), ((), ())), preferred_element_type=F32)

    edge = sx * DEPTH
    lane_n = lax.broadcasted_iota(jnp.int32, (labels, 2 * edge), 1)
    place = lane_n % edge
    north_ab = coefficients((place // DEPTH).astype(F32), (sy - DEPTH + place % DEPTH).astype(F32), lane_n < edge)
    y_of = sy - DEPTH + lax.broadcasted_iota(jnp.int32, (sy, 2 * edge), 1) % DEPTH
    pick = jnp.where(lax.broadcasted_iota(jnp.int32, (sy, 2 * edge), 0) == y_of, 1.0, 0.0).astype(BF16)
    spread_out = mm(region[...].astype(F32).astype(BF16), pick)
    x_of = (lax.broadcasted_iota(jnp.int32, (sx, 2 * edge), 1) % edge) // DEPTH
    own_row = lax.broadcasted_iota(jnp.int32, (sx, 2 * edge), 0) == x_of
    north_label = jnp.sum(jnp.where(own_row, spread_out, 0.0), axis=0, keepdims=True)
    north_mult = expand(jnp.where(north_label == lax.broadcasted_iota(jnp.int32, (labels, 2 * edge), 0).astype(F32), north_ab, 0.0))
    mn[0] = 1.0 + north_mult[:edge]
    mn[1] = north_mult[edge:]

    def mult_plane(x, carry):
        res = expand(jnp.where(reg2[pl.ds(x, 1), :] == label, ab[pl.ds(x, 1), :], 0.0))
        mult[0, x] = 1.0 + res[:sy]
        mult[1, x] = res[sy:]
        return carry

    for x in range(sx - DEPTH, sx):
        mult_plane(x, 0)

    def east_copy(t, p):
        return pltpu.make_async_remote_copy(
            src_ref=east_buf.at[t, :, pl.ds(2 * p, 2)], dst_ref=west_buf.at[t, :, pl.ds(2 * p, 2)],
            send_sem=send_e.at[t, p], recv_sem=recv_w.at[t, p],
            device_id=(a + 1, b), device_id_type=MESH)

    def north_copy(t):
        return pltpu.make_async_remote_copy(
            src_ref=north_buf.at[t], dst_ref=south_buf.at[t],
            send_sem=send_n.at[t], recv_sem=recv_s.at[t],
            device_id=(a, b + 1), device_id_type=MESH)

    def spread(q, even_in, odd_in, low, high):
        if high == DEPTH:
            cut = 2 * DEPTH * SUB
            outs = []
            for table, values, side in ((tee, even_in, 0), (toe, odd_in, 1)):
                total = None
                ends = []
                for k in range(2):
                    high_part, low_part = ln[2 * q + k, :, :span // 2], ln[2 * q + k, :, span // 2:]
                    lhs = jnp.concatenate([
                        table[...],
                        jnp.concatenate([high_part, high_part], axis=1),
                        jnp.concatenate([low_part, jnp.zeros_like(low_part)], axis=1)], axis=0)
                    out = mm(lhs, values[:, 2 * k * sz:2 * (k + 1) * sz])
                    ends.append(halves(out[:cut]))
                    part = halves(out[cut:])
                    total = part if total is None else total + part
                rows = pl.ds(side * edge // 2, edge // 2)
                nacc[rows, :] = total if q == 0 else nacc[rows, :] + total
                outs.append(jnp.concatenate(ends, axis=1))
            even, odd = outs
        else:
            rows = slice(low * SUB, high * SUB)
            even = mm(te[rows, :], jnp.concatenate([even_in, even_in[:span // 2]], axis=0))
            odd = mm(to[rows, :], jnp.concatenate([odd_in, odd_in[:span // 2]], axis=0))
        mirror = list(range(sx - 1 - low, sx - 1 - high, -1))
        if high == DEPTH:
            west_side[q] = even + odd
            res = even - odd
            held = mirror
        elif low == DEPTH:
            res = jnp.concatenate([west_side[q], even + odd, even - odd], axis=0)
            held = list(range(high)) + mirror
        else:
            res = jnp.concatenate([even + odd, even - odd], axis=0)
            held = list(range(high)) + mirror
        size = res.shape[0]
        done = along_z(jnp.concatenate([res[:, n * sz:(n + 1) * sz] for n in range(4)], axis=0), zz[...])
        for k in range(2):
            rows = pl.ds((2 * q + k) * SUB, SUB)
            for c in range(2):
                n = 2 * k + c
                block = done[n * size:(n + 1) * size].reshape(len(held), SUB, sz)
                for i, x in enumerate(held):
                    mid[c, x, rows, :] = block[i]

    zpad = jnp.zeros((SUB, sz), F32)

    for t in range(TICKS):
        west = west_in if t == 0 else west_buf.at[t - 1]
        south = south_in if t == 0 else south_buf.at[t - 1]
        def take_west():
            planes = []
            for j in range(DEPTH):
                plane = jnp.concatenate([west[0, j], west[1, j]], axis=1)
                planes.append(mm(ty[...], right3(plane)))
            rows = [q[:, c * sz:(c + 1) * sz] for c in range(2) for q in planes]
            done = along_z(jnp.concatenate(rows, axis=0), zz[...])
            wf[...] = done.reshape(2, DEPTH, sy, sz)

        if t > 0:
            @pl.when(has_s)
            def _():
                north_copy(t - 1).wait_recv()

            @pl.when(has_w)
            def _():
                for p in range(DEPTH // 2):
                    east_copy(t - 1, p).wait_recv()

        done = along_z(jnp.concatenate([south[0], south[1]], axis=0), zz[...])
        done = jnp.concatenate([done[:edge], done[edge:]], axis=1)
        rs[...] = right2(mm(ts[...], right3(done)))
        take_west()

        if t == 0:
            need("lsh", "lsl", "te", "to", "tee", "toe", "ln", "tn", "amp")

        source = t - a - b + (n_gx + n_gy - 2)
        live = jnp.where(slot[0, 0] == source, 1.0, 0.0).astype(F32)
        amps = (amp[0, source] * live, amp[1, source] * live)

        def spectrum(q):
            shared = mm(jnp.concatenate([lsh[q], lsh[q]], axis=1), rs[...])
            specs = []
            for k in range(2):
                g = 2 * q + k
                rows = pl.ds(g * SUB, SUB)
                p = point[rows, :]
                parts = []
                for c in range(2):
                    wh, wl = split(wf[c, :, rows, :].reshape(DEPTH * SUB, sz))
                    ph, pw = split(p * amps[c])
                    parts.append(jnp.concatenate([wh, wl, wh, ph, pw, ph, zpad], axis=0).astype(BF16))
                rw = jnp.concatenate([rs[: sx * DEPTH, :], jnp.concatenate(parts, axis=1)], axis=0)
                coeffs = shared[k * span:(k + 1) * span] + mm(jnp.concatenate([lsl[g], lw[...]], axis=1), rw)
                c0, c1 = coeffs[:, :sz], coeffs[:, sz:]
                pr, qr = pq[0, g], pq[1, g]
                specs += [c0 * pr + c1 * qr, c1 * pr - c0 * qr]
            spec = jnp.concatenate(specs, axis=1)
            return right2(spec[: span // 2]), right2(spec[span // 2:])

        if t + 1 == TICKS:
            ahead = spectrum(0)
            for q in range(groups // 2):
                even_in, odd_in = ahead
                if q + 1 < groups // 2:
                    ahead = spectrum(q + 1)
                spread(q, even_in, odd_in, 0, sx // 2)
            break

        for q in range(groups // 2):
            sp[2 * q], sp[2 * q + 1] = spectrum(q)
        for q in range(groups // 2):
            spread(q, sp[2 * q], sp[2 * q + 1], 0, DEPTH)


        def one_plane(x):
            fr, fi = finish_plane(x, mid, mult, ty)
            obuf[t, 0, x] = fr.astype(BF16)
            obuf[t, 1, x] = fi.astype(BF16)
            return fr, fi

        def east_planes(p):
            for j in range(2 * p, 2 * p + 2):
                field = one_plane(sx - DEPTH + j)
                for c in range(2):
                    east_buf[t, c, j] = field[c]

            @pl.when(has_e)
            def _():
                east_copy(t, p).start()

        if t == 0:
            @pl.when(jnp.logical_and(has_e, has_n))
            def _():
                pl.semaphore_wait(barrier, 2)

            @pl.when(jnp.logical_xor(has_e, has_n))
            def _():
                pl.semaphore_wait(barrier, 1)

        east_planes(0)
        back = mm(tn[...], right3(nacc[...]))
        back = along_z(jnp.concatenate([back[:, :sz], back[:, sz:]], axis=0), zz[...])
        re, im = back[:edge], back[edge:]
        north_buf[t, 0] = mn[0] * re - mn[1] * im
        north_buf[t, 1] = mn[0] * im + mn[1] * re
        east_planes(1)

        @pl.when(has_n)
        def _():
            north_copy(t).start()

        if t == 0:
            for x in range(sx - DEPTH):
                mult_plane(x, 0)

        for q in range(groups // 2):
            spread(q, sp[2 * q], sp[2 * q + 1], DEPTH, sx // 2)

        for x in range(sx - DEPTH):
            one_plane(x)

    for t in range(TICKS - 1):
        if t + 1 < TICKS:
            @pl.when(has_e)
            def _():
                for p in range(DEPTH // 2):
                    east_copy(t, p).wait_send()

            @pl.when(has_n)
            def _():
                north_copy(t).wait_send()


def solution(mesh):
    n_gx = mesh.shape["gx"]
    n_gy = mesh.shape["gy"]

    def local(west_in, south_in, region, pml_layers, vel_table, src_slot, src_cell, src_amp, wave_sq):
        sx, sy = region.shape
        sz = vel_table.shape[1]
        groups = sy // SUB
        consts = make_tables(sx, sy, sz)
        smem = pl.BlockSpec(memory_space=pltpu.SMEM)
        vmem = pl.BlockSpec(memory_space=pltpu.VMEM)
        hbm = pl.BlockSpec(memory_space=pl.ANY)
        dma = pltpu.SemaphoreType.DMA
        shape = (TICKS, 2, sx, sy, sz)
        inputs = [
            pml_layers.transpose(1, 2, 0).reshape(1, 4), src_amp, wave_sq.reshape(1, 1),
            west_in, south_in.reshape(2, sx * DEPTH, sz), region, vel_table,
            *[jnp.asarray(consts[name]) for name in NAMES],
        ]
        count = len(SCALARS)
        held = [pltpu.SMEM(v.shape, v.dtype) for v in inputs[:count]]
        held += [pltpu.VMEM(v.shape, v.dtype) for v in inputs[count:]]
        early, mid, mult = pl.pallas_call(
            functools.partial(kernel, n_gx, n_gy),
            out_shape=(
                pltpu.VMEM((TICKS - 1,) + shape[1:], BF16),
                pltpu.VMEM(shape[1:], F32),
                pltpu.VMEM(shape[1:], F32),
            ),
            in_specs=[smem] * 2 + [pl.BlockSpec(memory_space=pltpu.HBM)] * len(inputs),
            out_specs=(vmem,) * 3,
            scratch_shapes=held + [
                pltpu.VMEM((TICKS - 1, 2, DEPTH, sy, sz), F32),
                pltpu.VMEM((TICKS - 1, 2, sx * DEPTH, sz), F32),
                pltpu.VMEM((TICKS - 1, 2, DEPTH, sy, sz), F32),
                pltpu.VMEM((TICKS - 1, 2, sx * DEPTH, sz), F32),
                pltpu.VMEM(consts["lw"].shape, BF16),
                pltpu.VMEM((sy, sz), F32),
                pltpu.VMEM((2, groups, sx * SUB, sz), F32),
                pltpu.VMEM((sx, 2 * sy), jnp.int32),
                pltpu.VMEM((sx, 2 * sy), F32),
                pltpu.VMEM((2 * sx * DEPTH, 2 * sz), BF16),
                pltpu.VMEM((2, DEPTH, sy, sz), F32),
                pltpu.VMEM((groups, sx * SUB, 4 * sz), BF16),
                pltpu.VMEM((sx * DEPTH, 2 * sz), F32),
                pltpu.VMEM((2, sx * DEPTH, sz), F32),
                pltpu.VMEM((groups // 2, DEPTH * SUB, 4 * sz), F32),
                dma((TICKS - 1, DEPTH // 2)),
                dma((TICKS - 1, DEPTH // 2)),
                dma((TICKS - 1,)),
                dma((TICKS - 1,)),
                dma((len(inputs),)),
            ],
            compiler_params=pltpu.CompilerParams(
                collective_id=0, has_side_effects=True, vmem_limit_bytes=60000000),
        )(src_slot, src_cell, *inputs)
        keep = lambda v: pltpu.with_memory_space_constraint(v, pltpu.VMEM)
        return pl.pallas_call(
            finish,
            out_shape=jax.ShapeDtypeStruct(shape, BF16),
            in_specs=[vmem] * 4,
            out_specs=hbm,
            scratch_shapes=[pltpu.VMEM(shape[1:], BF16), dma((TICKS - 1 + PIECES,))],
            compiler_params=pltpu.CompilerParams(vmem_limit_bytes=16 * 1024 * 1024),
        )(keep(early), keep(mid), keep(mult), jnp.asarray(consts["ty"]))

    in_specs = (
        P(None, "gx", "gy", None),
        P(None, "gx", "gy", None),
        P("gx", "gy"),
        P(None, "gx", "gy"),
        P(),
        P("gx", "gy"),
        P("gx", "gy"),
        P(),
        P(),
    )
    out_specs = P(None, None, "gx", "gy", None)
    return jax.shard_map(local, mesh=mesh, in_specs=in_specs, out_specs=out_specs, check_vma=False)
```

```python
import functools

import jax
import jax.numpy as jnp
import numpy as np
from jax import lax
from jax.experimental import pallas as pl
from jax.experimental.pallas import tpu as pltpu
from jax.sharding import PartitionSpec as P

DEPTH = 4
TICKS = 3
PIECES = 2
SUB = 8
damping_ratio = 0.25
absorb_peak = 4.0
diagonal_base = 6.0
F32 = jnp.float32
BF16 = jnp.bfloat16
MESH = pl.DeviceIdType.MESH


def basis(count):
    k = np.arange(count, dtype=np.float64) + 1.0
    table = np.sqrt(2.0 / (count + 1.0)) * np.sin(np.pi * k[:, None] * k[None, :] / (count + 1.0))
    eigen = 2.0 - 2.0 * np.cos(np.pi * k / (count + 1.0))
    return table, eigen


def np_split(table):
    full = np.asarray(table, np.float32)
    high = full.astype(BF16)
    low = (full - high.astype(np.float32)).astype(BF16)
    return high, low


def left3(table):
    high, low = np_split(table)
    return np.concatenate([high, high, low], axis=1)


def fold(table):
    high, low = np_split(table)
    return np.concatenate([np.concatenate([high, high], 1), np.concatenate([low, np.zeros_like(low)], 1)], 0)


def split(values):
    high = values.astype(BF16).astype(F32)
    return high, values - high


def right3(values):
    high, low = split(values)
    high = high.astype(BF16)
    return jnp.concatenate([high, low.astype(BF16), high], axis=0)


def right2(values):
    high, low = split(values)
    return jnp.concatenate([high.astype(BF16), low.astype(BF16)], axis=0)


def mm(a, b):
    return jnp.dot(a, b, preferred_element_type=F32)


def halves(both):
    size = both.shape[0] // 2
    return both[:size] + both[size:]


def along_z(values, zz):
    high, low = split(values)
    both = jnp.concatenate([high.astype(BF16), low.astype(BF16)], axis=1)
    out = mm(both, zz)
    half = out.shape[1] // 2
    return out[:, :half] + out[:, half:]


def make_tables(sx, sy, sz):
    bx, ex = basis(sx)
    by, ey = basis(sy)
    bz, ez = basis(sz)
    eye = np.eye(SUB)
    groups = sy // SUB
    ls = [np_split(np.kron(np.eye(sx), by[g * SUB:(g + 1) * SUB, :DEPTH])) for g in range(groups)]
    lsh = np.stack([h for h, _ in ls])
    lsl = np.stack([low for _, low in ls])
    half = sx // 2
    order = np.concatenate([np.arange(0, sx, 2), np.arange(1, sx, 2)])
    bxo, exo = bx[order], ex[order]
    lw = left3(np.kron(bxo[:, :DEPTH], eye))
    lw = np.concatenate([lw, np.zeros((lw.shape[0], 4 * SUB), lw.dtype)], axis=1)
    even = np.kron(bx[:half, order[:half]], eye)
    odd = np.kron(bx[:half, order[half:]], eye)
    zh, zl = np_split(bz)
    zz = np.concatenate([np.concatenate([zh, zl], 1)] * 2, 0)
    return dict(
        lsh=lsh.reshape(groups // 2, -1, lsh.shape[2]),
        lsl=lsl,
        lw=lw,
        te=left3(even),
        to=left3(odd),
        tee=fold(even[:DEPTH * SUB]),
        toe=fold(odd[:DEPTH * SUB]),
        ln=np.stack([np.concatenate(np_split(np.kron(np.eye(half), by[sy - DEPTH:, g * SUB:(g + 1) * SUB])), axis=1) for g in range(groups)]),
        tn=left3(np.kron(bxo.T, np.eye(DEPTH))),
        ts=left3(np.kron(bxo, np.eye(DEPTH))),
        ty=left3(by),
        zz=zz,
        bxr=np.repeat(bxo, SUB, axis=0).astype(np.float32),
        byf=by.astype(np.float32),
        bzf=bz.astype(np.float32),
        exr=np.repeat(exo, SUB)[:, None].astype(np.float32) * np.ones((1, sz), np.float32),
        eyr=ey[:, None].astype(np.float32) * np.ones((1, sz), np.float32),
        ezr=ez[None, :].astype(np.float32),
    )


SCALARS = ("pml", "amp", "wave")
INVERSE_UNROLL = 8
NAMES = ("lsh", "lsl", "lw", "te", "to", "tee", "toe", "ln", "tn", "ts", "ty", "zz", "bxr", "byf", "bzf", "exr", "eyr", "ezr")


INPUTS = SCALARS + ("west_in", "south_in", "region", "vel") + NAMES
FIRST = ("wave", "ezr", "eyr", "exr", "bxr", "byf", "bzf", "lw", "pml", "region", "vel", "west_in", "south_in", "ty", "zz", "ts")
ORDER = FIRST + tuple(name for name in INPUTS if name not in FIRST)


def finish_plane(x, mid, mult, ty):
    sz = mid.shape[3]
    plane = jnp.concatenate([mid[0, x], mid[1, x]], axis=1)
    raw = mm(ty[...], right3(plane))
    re, im = raw[:, :sz], raw[:, sz:]
    mr, mi = mult[0, x], mult[1, x]
    fr = mr * re - mi * im
    fi = mr * im + mi * re
    return fr, fi


def finish(early, mid, mult, ty, out, last, sems):
    sx = mid.shape[1]
    count = early.shape[0]
    copies = [pltpu.make_async_copy(early, out.at[pl.ds(0, count)], sems.at[0])]
    for copy in copies:
        copy.start()
    size = sx // PIECES
    for k in range(PIECES):
        for x in range(k * size, (k + 1) * size):
            fr, fi = finish_plane(x, mid, mult, ty)
            last[0, x] = fr.astype(BF16)
            last[1, x] = fi.astype(BF16)
        part = pl.ds(k * size, size)
        copy = pltpu.make_async_copy(last.at[:, part], out.at[count, :, part], sems.at[count + k])
        copy.start()
        copies.append(copy)
    for copy in copies:
        copy.wait()


def kernel(n_gx, n_gy, *refs):
    slot, cell = refs[:2]
    outside, (obuf, mid, mult), refs = refs[2:27], refs[27:30], refs[30:]
    inside, refs = refs[:25], refs[25:]
    pml, amp, wave = inside[:3]
    (west_in, south_in, region, vel,
     lsh, lsl, lw0, te, to, tee, toe, ln, tn, ts, ty, zz, bxr, byf, bzf, exr, eyr, ezr) = inside[3:]
    (
     west_buf, south_buf, east_buf, north_buf,
     lw, point, pq, reg2, ab, rs, wf, sp, nacc, mn, west_side,
     send_e, recv_w, send_n, recv_s, load_sem) = refs
    sx, sy = region.shape
    sz = vel.shape[1]
    labels = vel.shape[0]
    groups = sy // SUB
    span = sx * SUB
    a = lax.axis_index("gx")
    b = lax.axis_index("gy")
    has_w, has_e = a > 0, a + 1 < n_gx
    has_s, has_n = b > 0, b + 1 < n_gy

    loads = {name: pltpu.make_async_copy(src, dst, load_sem.at[i])
             for i, (name, (src, dst)) in enumerate(zip(INPUTS, zip(outside, inside)))}
    for name in ORDER:
        loads[name].start()

    def need(*names):
        for name in names:
            loads[name].wait()

    barrier = pltpu.get_barrier_semaphore()

    @pl.when(has_w)
    def _():
        pl.semaphore_signal(barrier, inc=1, device_id=(a - 1, b), device_id_type=MESH)

    @pl.when(has_s)
    def _():
        pl.semaphore_signal(barrier, inc=1, device_id=(a, b - 1), device_id_type=MESH)


    @pl.when(jnp.logical_not(has_w))
    def _():
        west_buf[...] = jnp.zeros_like(west_buf)

    @pl.when(jnp.logical_not(has_s))
    def _():
        south_buf[...] = jnp.zeros_like(south_buf)

    need("wave", "exr", "eyr", "ezr", "bxr", "byf", "bzf", "lw", "pml", "region", "vel", "west_in", "south_in", "ty", "zz", "ts")
    w = wave[0, 0]
    damp = -damping_ratio * w

    def inverse_group(g, carry):
        y_part = eyr[pl.ds(pl.multiple_of(g * SUB, SUB), SUB), :]
        lam = exr[...].reshape(sx, SUB, sz) + y_part[None] + ezr[...][None] - w
        lam = lam.reshape(sx * SUB, sz)
        inv = 1.0 / (lam * lam + damp * damp)
        pq[0, g] = lam * inv
        pq[1, g] = damp * inv
        return carry

    lax.fori_loop(0, groups, inverse_group, 0, unroll=INVERSE_UNROLL)

    position = cell[0, 0]
    px = position // (sy * sz)
    py = (position // sz) % sy
    pz = position % sz
    x_lane = lax.broadcasted_iota(jnp.int32, (sx * SUB, sx), 1)
    bxp = jnp.sum(jnp.where(x_lane == px, bxr[...], 0.0), axis=1, keepdims=True)
    y_lane = lax.broadcasted_iota(jnp.int32, (sy, sy), 1)
    byp = jnp.sum(jnp.where(y_lane == py, byf[...], 0.0), axis=1, keepdims=True)
    z_row = lax.broadcasted_iota(jnp.int32, (sz, sz), 0)
    bzp = jnp.sum(jnp.where(z_row == pz, bzf[...], 0.0), axis=0, keepdims=True)
    point[...] = byp * bzp
    width = lw0.shape[1]
    first = 3 * DEPTH * SUB
    lane = lax.broadcasted_iota(jnp.int32, (sx * SUB, width), 1)
    row = lax.broadcasted_iota(jnp.int32, (sx * SUB, width), 0)
    xh, xl = split(bxp)
    dyn = jnp.where(lane < first + 2 * SUB, xh, xl)
    dyn = jnp.where((lane % SUB) == (row % SUB), dyn, 0.0)
    lw[...] = jnp.where(lane < first, lw0[...].astype(F32), dyn).astype(BF16)

    xi = lax.broadcasted_iota(jnp.int32, (sx, 2 * sy), 0).astype(F32)
    lane2 = lax.broadcasted_iota(jnp.int32, (sx, 2 * sy), 1)
    yi = (lane2 % sy).astype(F32)

    def ramp(i, distance):
        thick = pml[0, i].astype(F32)
        portion = jnp.maximum(thick - distance, 0.0) / jnp.maximum(jnp.full_like(distance, thick), 1.0)
        return portion * portion

    def coefficients(x, y, real):
        sigma = ramp(0, x) + ramp(1, sx - 1.0 - x) + ramp(2, y) + ramp(3, sy - 1.0 - y)
        sigma = absorb_peak * sigma
        return jnp.where(real, diagonal_base, -sigma) / (diagonal_base * diagonal_base + sigma * sigma)

    ab[...] = coefficients(xi, yi, lane2 < sy)
    reg2[...] = jnp.concatenate([region[...], region[...]], axis=1)
    ch, cl = split(vel[...] - w)
    contrast = jnp.concatenate([ch, ch, cl, cl], axis=0).astype(BF16)
    label = lax.broadcasted_iota(jnp.int32, (labels, 2 * sy), 0)

    def expand(own):
        oh, ol = split(own)
        lhs = jnp.concatenate([oh, ol, oh, ol], axis=0).astype(BF16)
        return lax.dot_general(lhs, contrast, (((0,), (0,)), ((), ())), preferred_element_type=F32)

    edge = sx * DEPTH
    lane_n = lax.broadcasted_iota(jnp.int32, (labels, 2 * edge), 1)
    place = lane_n % edge
    north_ab = coefficients((place // DEPTH).astype(F32), (sy - DEPTH + place % DEPTH).astype(F32), lane_n < edge)
    y_of = sy - DEPTH + lax.broadcasted_iota(jnp.int32, (sy, 2 * edge), 1) % DEPTH
    pick = jnp.where(lax.broadcasted_iota(jnp.int32, (sy, 2 * edge), 0) == y_of, 1.0, 0.0).astype(BF16)
    spread_out = mm(region[...].astype(F32).astype(BF16), pick)
    x_of = (lax.broadcasted_iota(jnp.int32, (sx, 2 * edge), 1) % edge) // DEPTH
    own_row = lax.broadcasted_iota(jnp.int32, (sx, 2 * edge), 0) == x_of
    north_label = jnp.sum(jnp.where(own_row, spread_out, 0.0), axis=0, keepdims=True)
    north_mult = expand(jnp.where(north_label == lax.broadcasted_iota(jnp.int32, (labels, 2 * edge), 0).astype(F32), north_ab, 0.0))
    mn[0] = 1.0 + north_mult[:edge]
    mn[1] = north_mult[edge:]

    def mult_plane(x, carry):
        res = expand(jnp.where(reg2[pl.ds(x, 1), :] == label, ab[pl.ds(x, 1), :], 0.0))
        mult[0, x] = 1.0 + res[:sy]
        mult[1, x] = res[sy:]
        return carry

    for x in range(sx - DEPTH, sx):
        mult_plane(x, 0)

    def east_copy(t, p):
        return pltpu.make_async_remote_copy(
            src_ref=east_buf.at[t, :, pl.ds(2 * p, 2)], dst_ref=west_buf.at[t, :, pl.ds(2 * p, 2)],
            send_sem=send_e.at[t, p], recv_sem=recv_w.at[t, p],
            device_id=(a + 1, b), device_id_type=MESH)

    def north_copy(t):
        return pltpu.make_async_remote_copy(
            src_ref=north_buf.at[t], dst_ref=south_buf.at[t],
            send_sem=send_n.at[t], recv_sem=recv_s.at[t],
            device_id=(a, b + 1), device_id_type=MESH)

    def spread(q, even_in, odd_in, low, high):
        if high == DEPTH:
            cut = 2 * DEPTH * SUB
            outs = []
            for table, values, side in ((tee, even_in, 0), (toe, odd_in, 1)):
                total = None
                ends = []
                for k in range(2):
                    high_part, low_part = ln[2 * q + k, :, :span // 2], ln[2 * q + k, :, span // 2:]
                    lhs = jnp.concatenate([
                        table[...],
                        jnp.concatenate([high_part, high_part], axis=1),
                        jnp.concatenate([low_part, jnp.zeros_like(low_part)], axis=1)], axis=0)
                    out = mm(lhs, values[:, 2 * k * sz:2 * (k + 1) * sz])
                    ends.append(halves(out[:cut]))
                    part = halves(out[cut:])
                    total = part if total is None else total + part
                rows = pl.ds(side * edge // 2, edge // 2)
                nacc[rows, :] = total if q == 0 else nacc[rows, :] + total
                outs.append(jnp.concatenate(ends, axis=1))
            even, odd = outs
        else:
            rows = slice(low * SUB, high * SUB)
            even = mm(te[rows, :], jnp.concatenate([even_in, even_in[:span // 2]], axis=0))
            odd = mm(to[rows, :], jnp.concatenate([odd_in, odd_in[:span // 2]], axis=0))
        mirror = list(range(sx - 1 - low, sx - 1 - high, -1))
        if high == DEPTH:
            west_side[q] = even + odd
            res = even - odd
            held = mirror
        elif low == DEPTH:
            res = jnp.concatenate([west_side[q], even + odd, even - odd], axis=0)
            held = list(range(high)) + mirror
        else:
            res = jnp.concatenate([even + odd, even - odd], axis=0)
            held = list(range(high)) + mirror
        size = res.shape[0]
        done = along_z(jnp.concatenate([res[:, n * sz:(n + 1) * sz] for n in range(4)], axis=0), zz[...])
        for k in range(2):
            rows = pl.ds((2 * q + k) * SUB, SUB)
            for c in range(2):
                n = 2 * k + c
                block = done[n * size:(n + 1) * size].reshape(len(held), SUB, sz)
                for i, x in enumerate(held):
                    mid[c, x, rows, :] = block[i]

    zpad = jnp.zeros((SUB, sz), F32)

    for t in range(TICKS):
        west = west_in if t == 0 else west_buf.at[t - 1]
        south = south_in if t == 0 else south_buf.at[t - 1]
        def take_west():
            planes = []
            for j in range(DEPTH):
                plane = jnp.concatenate([west[0, j], west[1, j]], axis=1)
                planes.append(mm(ty[...], right3(plane)))
            rows = [q[:, c * sz:(c + 1) * sz] for c in range(2) for q in planes]
            done = along_z(jnp.concatenate(rows, axis=0), zz[...])
            wf[...] = done.reshape(2, DEPTH, sy, sz)

        if t > 0:
            @pl.when(has_s)
            def _():
                north_copy(t - 1).wait_recv()

            @pl.when(has_w)
            def _():
                for p in range(DEPTH // 2):
                    east_copy(t - 1, p).wait_recv()

        done = along_z(jnp.concatenate([south[0], south[1]], axis=0), zz[...])
        done = jnp.concatenate([done[:edge], done[edge:]], axis=1)
        rs[...] = right2(mm(ts[...], right3(done)))
        take_west()

        if t == 0:
            need("lsh", "lsl", "te", "to", "tee", "toe", "ln", "tn", "amp")

        source = t - a - b + (n_gx + n_gy - 2)
        live = jnp.where(slot[0, 0] == source, 1.0, 0.0).astype(F32)
        amps = (amp[0, source] * live, amp[1, source] * live)

        def spectrum(q):
            shared = mm(jnp.concatenate([lsh[q], lsh[q]], axis=1), rs[...])
            specs = []
            for k in range(2):
                g = 2 * q + k
                rows = pl.ds(g * SUB, SUB)
                p = point[rows, :]
                parts = []
                for c in range(2):
                    wh, wl = split(wf[c, :, rows, :].reshape(DEPTH * SUB, sz))
                    ph, pw = split(p * amps[c])
                    parts.append(jnp.concatenate([wh, wl, wh, ph, pw, ph, zpad], axis=0).astype(BF16))
                rw = jnp.concatenate([rs[: sx * DEPTH, :], jnp.concatenate(parts, axis=1)], axis=0)
                coeffs = shared[k * span:(k + 1) * span] + mm(jnp.concatenate([lsl[g], lw[...]], axis=1), rw)
                c0, c1 = coeffs[:, :sz], coeffs[:, sz:]
                pr, qr = pq[0, g], pq[1, g]
                specs += [c0 * pr + c1 * qr, c1 * pr - c0 * qr]
            spec = jnp.concatenate(specs, axis=1)
            return right2(spec[: span // 2]), right2(spec[span // 2:])

        if t + 1 == TICKS:
            ahead = spectrum(0)
            for q in range(groups // 2):
                even_in, odd_in = ahead
                if q + 1 < groups // 2:
                    ahead = spectrum(q + 1)
                spread(q, even_in, odd_in, 0, sx // 2)
            break

        for q in range(groups // 2):
            sp[2 * q], sp[2 * q + 1] = spectrum(q)
        for q in range(groups // 2):
            spread(q, sp[2 * q], sp[2 * q + 1], 0, DEPTH)


        def one_plane(x):
            fr, fi = finish_plane(x, mid, mult, ty)
            obuf[t, 0, x] = fr.astype(BF16)
            obuf[t, 1, x] = fi.astype(BF16)
            return fr, fi

        def east_planes(p):
            for j in range(2 * p, 2 * p + 2):
                field = one_plane(sx - DEPTH + j)
                for c in range(2):
                    east_buf[t, c, j] = field[c]

            @pl.when(has_e)
            def _():
                east_copy(t, p).start()

        if t == 0:
            @pl.when(jnp.logical_and(has_e, has_n))
            def _():
                pl.semaphore_wait(barrier, 2)

            @pl.when(jnp.logical_xor(has_e, has_n))
            def _():
                pl.semaphore_wait(barrier, 1)

        east_planes(0)
        back = mm(tn[...], right3(nacc[...]))
        back = along_z(jnp.concatenate([back[:, :sz], back[:, sz:]], axis=0), zz[...])
        re, im = back[:edge], back[edge:]
        north_buf[t, 0] = mn[0] * re - mn[1] * im
        north_buf[t, 1] = mn[0] * im + mn[1] * re
        east_planes(1)

        @pl.when(has_n)
        def _():
            north_copy(t).start()

        if t == 0:
            for x in range(sx - DEPTH):
                mult_plane(x, 0)

        for q in range(groups // 2):
            spread(q, sp[2 * q], sp[2 * q + 1], DEPTH, sx // 2)

        for x in range(sx - DEPTH):
            one_plane(x)

    for t in range(TICKS - 1):
        if t + 1 < TICKS:
            @pl.when(has_e)
            def _():
                for p in range(DEPTH // 2):
                    east_copy(t, p).wait_send()

            @pl.when(has_n)
            def _():
                north_copy(t).wait_send()


def solution(mesh):
    n_gx = mesh.shape["gx"]
    n_gy = mesh.shape["gy"]

    def local(west_in, south_in, region, pml_layers, vel_table, src_slot, src_cell, src_amp, wave_sq):
        sx, sy = region.shape
        sz = vel_table.shape[1]
        groups = sy // SUB
        consts = make_tables(sx, sy, sz)
        smem = pl.BlockSpec(memory_space=pltpu.SMEM)
        vmem = pl.BlockSpec(memory_space=pltpu.VMEM)
        hbm = pl.BlockSpec(memory_space=pl.ANY)
        dma = pltpu.SemaphoreType.DMA
        shape = (TICKS, 2, sx, sy, sz)
        inputs = [
            pml_layers.transpose(1, 2, 0).reshape(1, 4), src_amp, wave_sq.reshape(1, 1),
            west_in, south_in.reshape(2, sx * DEPTH, sz), region, vel_table,
            *[jnp.asarray(consts[name]) for name in NAMES],
        ]
        count = len(SCALARS)
        held = [pltpu.SMEM(v.shape, v.dtype) for v in inputs[:count]]
        held += [pltpu.VMEM(v.shape, v.dtype) for v in inputs[count:]]
        early, mid, mult = pl.pallas_call(
            functools.partial(kernel, n_gx, n_gy),
            out_shape=(
                pltpu.VMEM((TICKS - 1,) + shape[1:], BF16),
                pltpu.VMEM(shape[1:], F32),
                pltpu.VMEM(shape[1:], F32),
            ),
            in_specs=[smem] * 2 + [pl.BlockSpec(memory_space=pltpu.HBM)] * len(inputs),
            out_specs=(vmem,) * 3,
            scratch_shapes=held + [
                pltpu.VMEM((TICKS - 1, 2, DEPTH, sy, sz), F32),
                pltpu.VMEM((TICKS - 1, 2, sx * DEPTH, sz), F32),
                pltpu.VMEM((TICKS - 1, 2, DEPTH, sy, sz), F32),
                pltpu.VMEM((TICKS - 1, 2, sx * DEPTH, sz), F32),
                pltpu.VMEM(consts["lw"].shape, BF16),
                pltpu.VMEM((sy, sz), F32),
                pltpu.VMEM((2, groups, sx * SUB, sz), F32),
                pltpu.VMEM((sx, 2 * sy), jnp.int32),
                pltpu.VMEM((sx, 2 * sy), F32),
                pltpu.VMEM((2 * sx * DEPTH, 2 * sz), BF16),
                pltpu.VMEM((2, DEPTH, sy, sz), F32),
                pltpu.VMEM((groups, sx * SUB, 4 * sz), BF16),
                pltpu.VMEM((sx * DEPTH, 2 * sz), F32),
                pltpu.VMEM((2, sx * DEPTH, sz), F32),
                pltpu.VMEM((groups // 2, DEPTH * SUB, 4 * sz), F32),
                dma((TICKS - 1, DEPTH // 2)),
                dma((TICKS - 1, DEPTH // 2)),
                dma((TICKS - 1,)),
                dma((TICKS - 1,)),
                dma((len(inputs),)),
            ],
            compiler_params=pltpu.CompilerParams(
                collective_id=0, has_side_effects=True, vmem_limit_bytes=60000000),
        )(src_slot, src_cell, *inputs)
        keep = lambda v: pltpu.with_memory_space_constraint(v, pltpu.VMEM)
        return pl.pallas_call(
            finish,
            out_shape=jax.ShapeDtypeStruct(shape, BF16),
            in_specs=[vmem] * 4,
            out_specs=hbm,
            scratch_shapes=[pltpu.VMEM(shape[1:], BF16), dma((TICKS - 1 + PIECES,))],
            compiler_params=pltpu.CompilerParams(vmem_limit_bytes=16 * 1024 * 1024),
        )(keep(early), keep(mid), keep(mult), jnp.asarray(consts["ty"]))

    in_specs = (
        P(None, "gx", "gy", None),
        P(None, "gx", "gy", None),
        P("gx", "gy"),
        P(None, "gx", "gy"),
        P(),
        P("gx", "gy"),
        P("gx", "gy"),
        P(),
        P(),
    )
    out_specs = P(None, None, "gx", "gy", None)
    return jax.shard_map(local, mesh=mesh, in_specs=in_specs, out_specs=out_specs, check_vma=False)
```
